256 devices in a mesh: dp: 8 (over y, core), expert: 32 (over x, z).
Axes of the slice: x: 4, y: 4, z: 8, core: 2. Of those that a mesh axis runs over, the one named last changes fastest.
Arguments:
- hidden_token_tiles: bfloat16 [8, 1024, 1024], P(None, 'dp'), may hold values from -6 to 6
- gradient_token_tiles: bfloat16 [8, 7168, 1024], P(None, 'expert', 'dp'), may hold values from -0.59765625 to 0.59765625
- momentum: float32 [8, 7168, 1024], P('dp', 'expert'), may hold values from -54 to 54, as said below
- filled_tile_count: int32 [8, 8], replicated, may hold values from 1 to 8, as said below
Outputs:
- new_momentum: float32 [8, 7168, 1024], P('dp', 'expert')
- update: float32 [8, 7168, 1024], P(None, 'expert')
The draws below stay inside these ranges and needn't reach their ends.
Inputs may be any that keep to these rules, and one draw needn't show every extreme that they name: momentum entries are finite reals. filled_tile_count[g, x] filled tiles stand at the head of group g's slots for expert x; in every draw one expert is full in every group.
All inputs are finite; a program needn't handle non-finite values.
Results may differ from the reference program's by a relative error of at most 0.0009.
Values may be sent and summed in bfloat16 or wider, within the bound.
No kernel may reach another device: no remote copies, remote signals or barrier semaphores. Data moves between devices by JAX's collectives and lax.ppermute only.
A program may use at most 64 MiB of HBM per device.

```python
import math
import jax
import jax.numpy as jnp
from jax import lax

D = 7168
FF = 1024
TILE = 16
TILES = 8
ITERS = 2
GROUPS = 8
EXPERTS = 8


def draw_momentum(key, part):
    key_rows = jax.random.fold_in(key, 11)
    key_cols = jax.random.fold_in(key, 12)
    key_base = jax.random.fold_in(key, 13)
    row_scale = jnp.exp(jax.random.uniform(key_rows, (EXPERTS, 1, FF), jnp.float32, math.log(0.3), math.log(3.0)))
    col_scale = jnp.exp(jax.random.uniform(key_cols, (EXPERTS, D, 1), jnp.float32, math.log(0.3), math.log(3.0)))
    base = jnp.clip(jax.random.normal(key_base, (EXPERTS, D, FF), jnp.float32), -6.0, 6.0)
    return (base * row_scale * col_scale).astype(jnp.float32)


def draw_filled_tile_count(key, part):
    key_counts = jax.random.fold_in(key, 21)
    key_full = jax.random.fold_in(key, 22)
    key_low = jax.random.fold_in(key, 23)
    group_random_key = jax.random.fold_in(key, 24)
    counts = jax.random.randint(key_counts, (GROUPS, EXPERTS), 1, TILES + 1)
    full_expert = jax.random.randint(key_full, (), 0, EXPERTS)
    low_expert = (full_expert + 1 + jax.random.randint(key_low, (), 0, EXPERTS - 1)) % EXPERTS
    low_group = jax.random.randint(group_random_key, (), 0, GROUPS)
    expert_iota = lax.broadcasted_iota(jnp.int32, (GROUPS, EXPERTS), 1)
    group_iota = lax.broadcasted_iota(jnp.int32, (GROUPS, EXPERTS), 0)
    counts = jnp.where(expert_iota == full_expert, TILES, counts)
    counts = jnp.where((expert_iota == low_expert) & (group_iota == low_group), 1, counts)
    return counts.astype(jnp.int32)


def raised(drawn, own_key, source, target, blocks, factor):
    def block_of(axis_at):
        return (jnp.arange(drawn.shape[axis_at]) // (drawn.shape[axis_at] // blocks)).reshape((-1,) + (1,) * (drawn.ndim - 1 - axis_at))

    first = jax.random.permutation(own_key, blocks)[block_of(target)]
    far = (block_of(target) + blocks // 2) % blocks
    return jnp.where((block_of(source) == first) | (block_of(source) == far), factor * drawn, drawn)


def block_scale(stream_key, dims, shards, smallest, top_value):
    level = 1.0
    for dim, shards_of in shards:
        heights = jax.random.uniform(jax.random.fold_in(jax.random.fold_in(stream_key, 6), dim), (shards_of,), jnp.float32, smallest / len(shards), top_value / len(shards))
        level = level * jnp.repeat(jnp.exp(heights), dims[dim] // shards_of).reshape((-1,) + (1,) * (len(dims) - 1 - dim))
    return level


def scatter_about(key, shape, scale, limit, shards=(), held_as=jnp.bfloat16):
    array = scale * jax.random.normal(key, shape, jnp.float32)
    if shards:
        array = array * block_scale(key, shape, shards, -0.22, 0.18)
    return jnp.clip(array, -limit, limit).astype(held_as)


def noise_with(rng, shape, spread, bound, shards, heavy, kind=jnp.bfloat16):
    result = spread * jax.random.normal(rng, shape, jnp.float32)
    if shards:
        result = result * block_scale(rng, shape, shards, -0.22, 0.18)
    return jnp.clip(raised(result, jax.random.fold_in(rng, 3), *heavy), -bound, bound).astype(kind)


def setup_inputs(seed: int = 0) -> dict:
    streams_of = jax.random.split(jax.random.key(seed), 5)
    return {
        "hidden_token_tiles": scatter_about(streams_of[0], (EXPERTS, GROUPS * TILES * TILE, FF), 1.0, 6.0, ((1, 8),)),
        "gradient_token_tiles": noise_with(streams_of[1], (EXPERTS, D, GROUPS * TILES * TILE), 0.1, 0.59765625, ((1, 32), (2, 8)), (2, 0, 8, 2.0)),
        "momentum": draw_momentum(jax.random.fold_in(streams_of[4], 71), 0),
        "filled_tile_count": draw_filled_tile_count(jax.random.fold_in(streams_of[4], 71), 0),
    }


MOMENTUM_DECAY = 0.95
EPSILON = 1e-07
COEF_A = 3.4445
COEF_B = -4.775
COEF_C = 2.0315

def full_dot(left, right):
    return jnp.dot(left, right, precision=lax.Precision.HIGHEST, preferred_element_type=jnp.float32)

def reference(hidden_token_tiles, gradient_token_tiles, momentum, filled_tile_count):
    rows_group = TILES * TILE
    positions = jnp.arange(GROUPS * rows_group, dtype=jnp.int32)
    group_of_rows = positions // rows_group
    within = positions % rows_group
    factor = math.sqrt(max(FF, D))

    def one_expert(index):
        limits = filled_tile_count[:, index] * TILE
        tallied_tiles = within < limits[group_of_rows]
        retained_entries = jnp.where(tallied_tiles[:, None], hidden_token_tiles[index], jnp.zeros((), jnp.bfloat16))
        gradient = jnp.dot(gradient_token_tiles[index], retained_entries, preferred_element_type=jnp.float32)
        moment = MOMENTUM_DECAY * momentum[index] + gradient
        length = jnp.sqrt(jnp.sum(moment * moment))
        current = moment / (length + EPSILON)
        for iteration in range(ITERS):
            gram_matrix = full_dot(current.T, current)
            mixer = COEF_B * gram_matrix + COEF_C * full_dot(gram_matrix, gram_matrix)
            current = COEF_A * current + full_dot(current, mixer)
        return (moment, current * factor)
    moments, muon_updates = lax.map(one_expert, jnp.arange(EXPERTS, dtype=jnp.int32))
    return (moments, muon_updates)
```

```python
import math

import jax
import jax.numpy as jnp
from jax import lax
from jax.experimental import pallas as pl
from jax.experimental.pallas import tpu as pltpu
from jax.sharding import PartitionSpec as P

D = 7168
FF = 1024
TILE = 16
BLOCK = 128
UNIT = 16

MOMENTUM_DECAY = 0.95
EPSILON = 1e-07
COEF_A = 3.4445
COEF_B = -4.775
COEF_C = 2.0315

BF16 = jnp.bfloat16
F32 = jnp.float32


def split_two(value):
    high = value.astype(BF16)
    return high, (value - high.astype(F32)).astype(BF16)


def block_pairs():
    count = FF // BLOCK
    return [(i, j) for i in range(count) for j in range(i, count)]


def gram_kernel(counts_ref, tokens_ref, hidden_ref, momentum_ref, moment_ref, packed_ref):
    groups, _, width = tokens_ref.shape
    lanes = lax.broadcasted_iota(jnp.int32, tokens_ref.shape[1:], 1)
    tokens = jnp.concatenate(
        [
            jnp.where(lanes < counts_ref[g] * TILE, tokens_ref[g].astype(F32), 0.0).astype(BF16)
            for g in range(groups)
        ],
        axis=1,
    )
    hidden = hidden_ref[...].reshape(groups * width, FF)
    gradient = jnp.dot(tokens, hidden, preferred_element_type=F32)
    moment = MOMENTUM_DECAY * momentum_ref[...] + gradient
    moment_ref[...] = moment

    high, low = split_two(moment)
    left = jnp.concatenate([high, low, high], axis=0).T
    right = jnp.concatenate([high, high, low], axis=0)
    per_device = packed_ref.shape[1] // UNIT - 1
    unit = 0
    for i in range(FF // BLOCK):
        strip = jnp.dot(
            left[i * BLOCK : (i + 1) * BLOCK], right[:, i * BLOCK :], preferred_element_type=F32
        ).astype(BF16)
        for j in range(i, FF // BLOCK):
            block = strip[:, (j - i) * BLOCK : (j - i + 1) * BLOCK]
            for k in range(BLOCK // UNIT):
                device, place = divmod(unit, per_device)
                packed_ref[device, place * UNIT : (place + 1) * UNIT, :] = block[
                    k * UNIT : (k + 1) * UNIT
                ]
                unit += 1

    total = jnp.sum(jnp.sum(moment * moment, axis=0, keepdims=True), axis=1, keepdims=True)
    first = total.astype(BF16).astype(F32)
    second = (total - first).astype(BF16).astype(F32)
    third = total - first - second
    rows = lax.broadcasted_iota(jnp.int32, (UNIT, BLOCK), 0)
    tile = jnp.where(rows == 0, first, jnp.where(rows == 1, second, jnp.where(rows == 2, third, 0.0)))
    for device in range(packed_ref.shape[0]):
        packed_ref[device, per_device * UNIT :, :] = tile.astype(BF16)


def sum_kernel(parts_ref, copies_ref, factor_ref):
    devices = parts_ref.shape[0]
    rows = copies_ref.shape[1]
    total = parts_ref[0].astype(F32)
    for source in range(1, devices):
        total = total + parts_ref[source].astype(F32)
    squares = jnp.sum(total[rows:], axis=0, keepdims=True)
    factor = 1.0 / (jnp.sqrt(squares) + EPSILON)
    piece = (total[:rows] * factor * factor).astype(BF16)
    for target in range(devices):
        copies_ref[target] = piece
    factor_ref[...] = jnp.broadcast_to(factor, factor_ref.shape)


def polynomial_kernel(moment_ref, factor_ref, packed_ref, update_ref, gram_ref):
    packed = packed_ref[...].reshape(-1, BLOCK)
    for at, (i, j) in enumerate(block_pairs()):
        block = packed[at * BLOCK : (at + 1) * BLOCK]
        gram_ref[i * BLOCK : (i + 1) * BLOCK, j * BLOCK : (j + 1) * BLOCK] = block
        if i != j:
            gram_ref[j * BLOCK : (j + 1) * BLOCK, i * BLOCK : (i + 1) * BLOCK] = block.T

    def by_gram(value):
        rows = value.shape[0]
        both = jnp.dot(
            jnp.concatenate(split_two(value), axis=0), gram_ref[...], preferred_element_type=F32
        )
        return both[:rows] + both[rows:]

    def by_first(value):
        return COEF_A * value + by_gram(COEF_B * value + COEF_C * by_gram(value))

    def by_second_gram(value):
        return by_first(by_gram(by_first(value)))

    start = moment_ref[...] * factor_ref[0:1, 0:1]
    once = by_first(start)
    twice = COEF_A * once + by_second_gram(COEF_B * once + COEF_C * by_second_gram(once))
    update_ref[...] = twice * math.sqrt(max(FF, D))


def whole(memory_space=pltpu.VMEM):
    return pl.BlockSpec(memory_space=memory_space)


PARAMS = pltpu.CompilerParams(vmem_limit_bytes=48 * 1024 * 1024)


def body(hidden_token_tiles, gradient_token_tiles, momentum, filled_tile_count):
    group = lax.axis_index("dp")
    devices = lax.axis_size("expert")
    rows = momentum.shape[1]
    piece = len(block_pairs()) * BLOCK // devices
    counts = lax.dynamic_index_in_dim(filled_tile_count, group, 1, keepdims=False)
    tokens = lax.all_to_all(gradient_token_tiles, "dp", 0, 0, tiled=True)
    hidden = lax.all_to_all(hidden_token_tiles, "dp", 0, 0, tiled=True)
    moment, packed = pl.pallas_call(
        gram_kernel,
        out_shape=(
            jax.ShapeDtypeStruct((rows, FF), F32),
            jax.ShapeDtypeStruct((devices, piece + UNIT, BLOCK), BF16),
        ),
        in_specs=[whole(pltpu.SMEM), whole(), whole(), whole()],
        out_specs=(whole(), whole()),
        compiler_params=PARAMS,
        name="gram",
    )(counts, tokens, hidden, momentum[0])
    parts = lax.all_to_all(packed, "expert", 0, 0, tiled=True)
    copies, factor = pl.pallas_call(
        sum_kernel,
        out_shape=(
            jax.ShapeDtypeStruct((devices, piece, BLOCK), BF16),
            jax.ShapeDtypeStruct((8, BLOCK), F32),
        ),
        in_specs=[whole()],
        out_specs=(whole(), whole()),
        compiler_params=PARAMS,
        name="total",
    )(parts)
    gram = lax.all_to_all(copies, "expert", 0, 0, tiled=True)
    update = pl.pallas_call(
        polynomial_kernel,
        out_shape=jax.ShapeDtypeStruct((rows, FF), F32),
        in_specs=[whole(), whole(), whole()],
        out_specs=whole(),
        scratch_shapes=[pltpu.VMEM((FF, FF), BF16)],
        compiler_params=PARAMS,
        name="polynomial",
    )(moment, factor, gram)
    gathered = lax.all_gather((update * 256.0).astype(jnp.float16), "dp", axis=0, tiled=False)
    return (moment[None], gathered.astype(F32) * (1.0 / 256.0))


def solution(mesh):
    placed = (P(None, "dp", None), P(None, "expert", "dp"), P("dp", "expert", None), P())
    return jax.shard_map(
        body,
        mesh=mesh,
        in_specs=placed,
        out_specs=(P("dp", "expert", None), P(None, "expert", None)),
        check_vma=False,
    )
```

```python
import math

import jax
import jax.numpy as jnp
from jax import lax
from jax.experimental import pallas as pl
from jax.experimental.pallas import tpu as pltpu
from jax.sharding import Mesh
from jax.sharding import PartitionSpec as P

D = 7168
FF = 1024
TILE = 16
BLOCK = 128
UNIT = 16

MOMENTUM_DECAY = 0.95
EPSILON = 1e-07
COEF_A = 3.4445
COEF_B = -4.775
COEF_C = 2.0315

DP = ("y", "core")
EXPERT = ("x", "z")

BF16 = jnp.bfloat16
F32 = jnp.float32


def split_two(value):
    high = value.astype(BF16)
    return high, (value - high.astype(F32)).astype(BF16)


def block_pairs():
    count = FF // BLOCK
    return [(i, j) for i in range(count) for j in range(i, count)]


def pieces_of(total, shape):
    first = total.astype(BF16).astype(F32)
    second = (total - first).astype(BF16).astype(F32)
    third = total - first - second
    rows = lax.broadcasted_iota(jnp.int32, shape, 0)
    tile = jnp.where(rows == 0, first, jnp.where(rows == 1, second, jnp.where(rows == 2, third, 0.0)))
    return tile.astype(BF16)


def pack_kernel(counts_ref, hidden_ref, tokens_ref, packed_ref):
    lanes = lax.broadcasted_iota(jnp.int32, tokens_ref.shape[1:], 1)
    for x in range(hidden_ref.shape[0]):
        for c in range(FF // BLOCK):
            packed_ref[x, c * BLOCK : (c + 1) * BLOCK] = hidden_ref[x, :, c * BLOCK : (c + 1) * BLOCK]
        kept = jnp.where(lanes < counts_ref[x] * TILE, tokens_ref[x].astype(F32), 0.0)
        packed_ref[x, FF:] = kept.astype(BF16)


def gram_kernel(place_ref, tiles_ref, momentum_ref, moment_ref, packed_ref):
    groups = tiles_ref.shape[0]
    tokens = jnp.concatenate([tiles_ref[g, FF:] for g in range(groups)], axis=1)
    hidden = jnp.concatenate(
        [
            jnp.concatenate([tiles_ref[g, c * BLOCK : (c + 1) * BLOCK] for c in range(FF // BLOCK)], axis=1)
            for g in range(groups)
        ],
        axis=0,
    )
    gradient = jnp.dot(tokens, hidden, preferred_element_type=F32)
    moment = MOMENTUM_DECAY * momentum_ref[...] + gradient
    moment_ref[...] = moment

    high, low = split_two(moment)
    left = jnp.concatenate([high, low, high], axis=0).T
    right = jnp.concatenate([high, high, low], axis=0)
    chunks = packed_ref.shape[0]
    per_chunk = len(block_pairs()) // chunks
    at = 0
    for i in range(FF // BLOCK):
        strip = jnp.dot(
            left[i * BLOCK : (i + 1) * BLOCK], right[:, i * BLOCK :], preferred_element_type=F32
        ).astype(BF16)
        for j in range(i, FF // BLOCK):
            chunk, place = divmod(at, per_chunk)
            packed_ref[
                lax.rem(chunk - place_ref[0] + chunks, chunks), place * BLOCK : (place + 1) * BLOCK, :
            ] = strip[:, (j - i) * BLOCK : (j - i + 1) * BLOCK]
            at += 1

    total = jnp.sum(jnp.sum(moment * moment, axis=0, keepdims=True), axis=1, keepdims=True)
    tile = pieces_of(total, (UNIT, BLOCK))
    for chunk in range(chunks):
        packed_ref[chunk, per_chunk * BLOCK :, :] = tile


def middle_kernel(own_ref, *refs):
    *others, cut_ref = refs
    targets, height, _ = cut_ref.shape
    rows = height - UNIT
    total = own_ref[...].astype(F32)
    for other in others:
        total = total + other[...].astype(F32)
    tile = pieces_of(jnp.sum(total[targets * rows :, 0:1], axis=0, keepdims=True), (UNIT, BLOCK))
    for target in range(targets):
        cut_ref[target, :rows] = total[target * rows : (target + 1) * rows].astype(BF16)
        cut_ref[target, rows:] = tile


def sum_kernel(parts_ref, copies_ref, factor_ref):
    devices = parts_ref.shape[0]
    rows = copies_ref.shape[1]
    total = parts_ref[0].astype(F32)
    for source in range(1, devices):
        total = total + parts_ref[source].astype(F32)
    squares = jnp.sum(total[rows:], axis=0, keepdims=True)
    factor = 1.0 / (jnp.sqrt(squares) + EPSILON)
    piece = (total[:rows] * factor * factor).astype(BF16)
    for target in range(devices):
        copies_ref[target] = piece
    factor_ref[...] = jnp.broadcast_to(factor, factor_ref.shape)


def polynomial_kernel(place_ref, moment_ref, factor_ref, *refs):
    *chunk_refs, update_ref, packed_ref, gram_ref = refs
    chunks = len(chunk_refs)
    for distance, chunk_ref in enumerate(chunk_refs):
        packed_ref[lax.rem(place_ref[0] - distance + chunks, chunks)] = chunk_ref[...]
    per_chunk = len(block_pairs()) // chunks
    for at, (i, j) in enumerate(block_pairs()):
        chunk, place = divmod(at, per_chunk)
        block = packed_ref[chunk, place * BLOCK : (place + 1) * BLOCK]
        gram_ref[i * BLOCK : (i + 1) * BLOCK, j * BLOCK : (j + 1) * BLOCK] = block
        if i != j:
            gram_ref[j * BLOCK : (j + 1) * BLOCK, i * BLOCK : (i + 1) * BLOCK] = block.T

    def by_gram(value):
        rows = value.shape[0]
        both = jnp.dot(
            jnp.concatenate(split_two(value), axis=0), gram_ref[...], preferred_element_type=F32
        )
        return both[:rows] + both[rows:]

    def by_first(value):
        return COEF_A * value + by_gram(COEF_B * value + COEF_C * by_gram(value))

    def by_second_gram(value):
        return by_first(by_gram(by_first(value)))

    start = moment_ref[...] * factor_ref[0:1, 0:1]
    once = by_first(start)
    twice = COEF_A * once + by_second_gram(COEF_B * once + COEF_C * by_second_gram(once))
    update_ref[...] = twice * math.sqrt(max(FF, D))


def whole(memory_space=pltpu.VMEM):
    return pl.BlockSpec(memory_space=memory_space)


PARAMS = pltpu.CompilerParams(vmem_limit_bytes=48 * 1024 * 1024)


def call(kernel, out_shape, inputs, scratch=(), scalars=0):
    return pl.pallas_call(
        kernel,
        out_shape=out_shape,
        in_specs=[whole(pltpu.SMEM)] * scalars + [whole()] * (len(inputs) - scalars),
        out_specs=jax.tree.map(lambda _: whole(), out_shape),
        scratch_shapes=scratch,
        compiler_params=PARAMS,
        name=kernel.__name__.removesuffix("_kernel"),
    )(*inputs)


def shifted(value, axis, distance):
    size = lax.axis_size(axis)
    return lax.ppermute(value, axis, [(i, (i + distance) % size) for i in range(size)])


def body(hidden_token_tiles, gradient_token_tiles, momentum, filled_tile_count):
    experts = hidden_token_tiles.shape[0]
    along_x, along_z = lax.axis_size("x"), lax.axis_size("z")
    rows = momentum.shape[1]
    chunk = len(block_pairs()) * BLOCK // along_x
    piece = chunk // along_z
    counts = lax.dynamic_index_in_dim(filled_tile_count, lax.axis_index(DP), 0, keepdims=False)
    place = lax.axis_index("x").astype(jnp.int32).reshape(1)

    packed = call(
        pack_kernel,
        jax.ShapeDtypeStruct((experts, FF + rows, BLOCK), BF16),
        (counts, hidden_token_tiles, gradient_token_tiles),
        scalars=1,
    )
    tiles = lax.all_to_all(packed, DP, 0, 0, tiled=True)
    moment, parts = call(
        gram_kernel,
        (
            jax.ShapeDtypeStruct((rows, FF), F32),
            jax.ShapeDtypeStruct((along_x, chunk + UNIT, BLOCK), BF16),
        ),
        (place, tiles, momentum[0]),
        scalars=1,
    )
    cut = call(
        middle_kernel,
        jax.ShapeDtypeStruct((along_z, piece + UNIT, BLOCK), BF16),
        [parts[0]] + [shifted(parts[k], "x", k) for k in range(1, along_x)],
    )
    copies, factor = call(
        sum_kernel,
        (
            jax.ShapeDtypeStruct((along_z, piece, BLOCK), BF16),
            jax.ShapeDtypeStruct((8, BLOCK), F32),
        ),
        [lax.all_to_all(cut, "z", 0, 0, tiled=True)],
    )
    own = lax.all_to_all(copies, "z", 0, 0, tiled=True).reshape(chunk, BLOCK)
    update = call(
        polynomial_kernel,
        jax.ShapeDtypeStruct((rows, FF), F32),
        [place, moment, factor, own] + [shifted(own, "x", k) for k in range(1, along_x)],
        scratch=[pltpu.VMEM((along_x, chunk, BLOCK), BF16), pltpu.VMEM((FF, FF), BF16)],
        scalars=1,
    )
    gathered = lax.all_gather((update * 256.0).astype(jnp.float16), DP, axis=0, tiled=False)
    return (moment[None], gathered.astype(F32) * (1.0 / 256.0))


def solution(mesh):
    split = Mesh(mesh.devices.reshape(4, 2, 4, 8), ("y", "core", "x", "z"))
    placed = (P(None, DP, None), P(None, EXPERT, DP), P(DP, EXPERT, None), P())
    return jax.shard_map(
        body,
        mesh=split,
        in_specs=placed,
        out_specs=(P(DP, EXPERT, None), P(None, EXPERT, None)),
        check_vma=False,
    )
```

```python
import math

import jax
import jax.numpy as jnp
from jax import lax
from jax.experimental import pallas as pl
from jax.experimental.pallas import tpu as pltpu
from jax.sharding import Mesh
from jax.sharding import PartitionSpec as P

D = 7168
FF = 1024
TILE = 16
BLOCK = 128
UNIT = 16
NEEDED = 6

MOMENTUM_DECAY = 0.95
EPSILON = 1e-07
COEF_A = 3.4445
COEF_B = -4.775
COEF_C = 2.0315

DP = ("y", "core")
EXPERT = ("x", "z")

BF16 = jnp.bfloat16
F32 = jnp.float32


def split_two(value):
    high = value.astype(BF16)
    return high, (value - high.astype(F32)).astype(BF16)


def block_pairs(place):
    half = 0 if place < 2 else 1
    return [(0, 0), (0, 1), (0, 2), (0, 3), (0, 5), (1, 1), (1, 2), (1, 3), (half, 4 + half)]


def pieces_of(total, shape):
    first = total.astype(BF16).astype(F32)
    second = (total - first).astype(BF16).astype(F32)
    third = total - first - second
    rows = lax.broadcasted_iota(jnp.int32, shape, 0)
    tile = jnp.where(rows == 0, first, jnp.where(rows == 1, second, jnp.where(rows == 2, third, 0.0)))
    return tile.astype(BF16)


def column(place, block):
    return pl.ds(pl.multiple_of(lax.rem(2 * place + block, FF // BLOCK) * BLOCK, BLOCK), BLOCK)


def columns_kernel(place_ref, momentum_ref, *column_refs):
    for distance, column_ref in enumerate(column_refs, 1):
        for block in range(NEEDED):
            value = momentum_ref[:, column(place_ref[0] + distance, block)]
            column_ref[:, block * BLOCK : (block + 1) * BLOCK] = value.astype(BF16)


def gram_kernel(place_ref, counts_ref, hidden_ref, momentum_ref, tokens_ref, *refs):
    *other_refs, moment_ref, cut_ref, needed_ref = refs
    groups, height, width = tokens_ref.shape
    place = place_ref[0]
    lanes = lax.broadcasted_iota(jnp.int32, (height, width), 1)

    def tokens_of(ref):
        kept = [jnp.where(lanes < counts_ref[g] * TILE, ref[g].astype(F32), 0.0) for g in range(groups)]
        return jnp.concatenate(kept, axis=1).astype(BF16)

    gradient = jnp.dot(
        tokens_of(tokens_ref), hidden_ref[...].reshape(groups * width, FF), preferred_element_type=F32
    )
    moment = MOMENTUM_DECAY * momentum_ref[...] + gradient
    moment_ref[...] = moment

    for g in range(groups):
        for block in range(NEEDED):
            needed_ref[g * width : (g + 1) * width, block * BLOCK : (block + 1) * BLOCK] = hidden_ref[
                g, :, column(place, block)
            ]
    values = [jnp.concatenate([moment_ref[:, column(place, block)] for block in range(NEEDED)], axis=1)]
    others = len(other_refs) // 2
    for momentum_columns, other_tokens in zip(other_refs[:others], other_refs[others:]):
        gradient = jnp.dot(tokens_of(other_tokens), needed_ref[...], preferred_element_type=F32)
        values.append(MOMENTUM_DECAY * momentum_columns[...].astype(F32) + gradient)
    high, low = split_two(jnp.concatenate(values, axis=0))
    left = jnp.concatenate([high[:, : 2 * BLOCK], low[:, : 2 * BLOCK], high[:, : 2 * BLOCK]], axis=0).T
    right = jnp.concatenate([high, high, low], axis=0)
    strips = [
        jnp.dot(left[i * BLOCK : (i + 1) * BLOCK], right, preferred_element_type=F32).astype(BF16)
        for i in range(2)
    ]

    def block_of(i, j):
        return strips[i][:, j * BLOCK : (j + 1) * BLOCK]

    blocks = [block_of(i, j) for i, j in block_pairs(0)[:-1]]
    blocks.append(jnp.where(place < 2, block_of(*block_pairs(0)[-1]), block_of(*block_pairs(2)[-1])))
    per_device = cut_ref.shape[1] // UNIT - 1
    for unit in range(cut_ref.shape[0] * per_device):
        device, at = divmod(unit, per_device)
        block, row = divmod(unit * UNIT, BLOCK)
        cut_ref[device, at * UNIT : (at + 1) * UNIT] = blocks[block][row : row + UNIT]
    total = jnp.sum(jnp.sum(moment * moment, axis=0, keepdims=True), axis=1, keepdims=True)
    for device in range(cut_ref.shape[0]):
        cut_ref[device, per_device * UNIT :] = pieces_of(total, (UNIT, BLOCK))


def sum_kernel(parts_ref, copies_ref):
    total = parts_ref[0].astype(F32)
    for source in range(1, parts_ref.shape[0]):
        total = total + parts_ref[source].astype(F32)
    rows = total.shape[0] - UNIT
    squares = jnp.sum(total[rows:, 0:1], axis=0, keepdims=True)
    piece = total[:rows].astype(BF16)
    tile = pieces_of(squares, (UNIT, BLOCK))
    for target in range(copies_ref.shape[0]):
        copies_ref[target, :rows] = piece
        copies_ref[target, rows:] = tile


def polynomial_kernel(place_ref, moment_ref, *refs):
    *chunk_refs, update_ref, packed_ref, gram_ref = refs
    chunks = len(chunk_refs)
    pieces, height, _ = chunk_refs[0].shape
    rows = height - UNIT
    squares = jnp.zeros((1, 1), F32)
    for distance, chunk_ref in enumerate(chunk_refs):
        source = lax.rem(place_ref[0] - distance + chunks, chunks)
        for piece in range(pieces):
            packed_ref[source, piece * rows : (piece + 1) * rows] = chunk_ref[piece, :rows]
        squares = squares + jnp.sum(chunk_ref[0, rows:].astype(F32)[:, 0:1], axis=0, keepdims=True)
    factor = 1.0 / (jnp.sqrt(squares) + EPSILON)
    for source in range(chunks):
        for at, pair in enumerate(block_pairs(source)):
            i, j = ((2 * source + block) % (FF // BLOCK) for block in pair)
            block = packed_ref[source, at * BLOCK : (at + 1) * BLOCK]
            gram_ref[i * BLOCK : (i + 1) * BLOCK, j * BLOCK : (j + 1) * BLOCK] = block
            if i != j:
                gram_ref[j * BLOCK : (j + 1) * BLOCK, i * BLOCK : (i + 1) * BLOCK] = block.T

    def by_gram(value):
        rows = value.shape[0]
        both = jnp.dot(
            jnp.concatenate(split_two(value), axis=0), gram_ref[...], preferred_element_type=F32
        )
        return (both[:rows] + both[rows:]) * factor * factor

    def by_first(value):
        return COEF_A * value + by_gram(COEF_B * value + COEF_C * by_gram(value))

    def by_second_gram(value):
        return by_first(by_gram(by_first(value)))

    once = by_first(moment_ref[...] * factor)
    twice = COEF_A * once + by_second_gram(COEF_B * once + COEF_C * by_second_gram(once))
    update_ref[...] = twice * math.sqrt(max(FF, D))


def whole(memory_space=pltpu.VMEM):
    return pl.BlockSpec(memory_space=memory_space)


PARAMS = pltpu.CompilerParams(vmem_limit_bytes=48 * 1024 * 1024)


def call(kernel, out_shape, inputs, scratch=(), scalars=0):
    return pl.pallas_call(
        kernel,
        out_shape=out_shape,
        in_specs=[whole(pltpu.SMEM)] * scalars + [whole()] * (len(inputs) - scalars),
        out_specs=jax.tree.map(lambda _: whole(), out_shape),
        scratch_shapes=scratch,
        compiler_params=PARAMS,
        name=kernel.__name__.removesuffix("_kernel"),
    )(*inputs)


def shifted(value, axis, distance):
    size = lax.axis_size(axis)
    return lax.ppermute(value, axis, [(i, (i + distance) % size) for i in range(size)])


def body(hidden_token_tiles, gradient_token_tiles, momentum, filled_tile_count):
    along_x, along_z = lax.axis_size("x"), lax.axis_size("z")
    rows = momentum.shape[1]
    piece = len(block_pairs(0)) * BLOCK // along_z
    counts = lax.dynamic_index_in_dim(filled_tile_count, lax.axis_index(DP), 1, keepdims=False)
    place = lax.axis_index("x").astype(jnp.int32).reshape(1)
    distances = range(1, along_x)

    columns = call(
        columns_kernel,
        [jax.ShapeDtypeStruct((rows, NEEDED * BLOCK), BF16) for _ in distances],
        [place, momentum[0]],
        scalars=1,
    )
    other_columns = [shifted(columns[k - 1], "x", k) for k in distances]
    tokens = lax.all_to_all(gradient_token_tiles, DP, 0, 0, tiled=True)
    other_tokens = [shifted(tokens, "x", k) for k in distances]
    hidden = lax.all_to_all(hidden_token_tiles, DP, 0, 0, tiled=True)
    moment, cut = call(
        gram_kernel,
        (
            jax.ShapeDtypeStruct((rows, FF), F32),
            jax.ShapeDtypeStruct((along_z, piece + UNIT, BLOCK), BF16),
        ),
        [place, counts, hidden, momentum[0], tokens] + other_columns + other_tokens,
        scratch=[pltpu.VMEM((hidden.shape[0] * hidden.shape[1], NEEDED * BLOCK), BF16)],
        scalars=2,
    )
    copies = call(
        sum_kernel,
        jax.ShapeDtypeStruct((along_z, piece + UNIT, BLOCK), BF16),
        [lax.all_to_all(cut, "z", 0, 0, tiled=True)],
    )
    own = lax.all_to_all(copies, "z", 0, 0, tiled=True)
    update = call(
        polynomial_kernel,
        jax.ShapeDtypeStruct((rows, FF), F32),
        [place, moment, own] + [shifted(own, "x", k) for k in distances],
        scratch=[
            pltpu.VMEM((along_x, along_z * piece, BLOCK), BF16),
            pltpu.VMEM((FF, FF), BF16),
        ],
        scalars=1,
    )
    gathered = lax.all_gather((update * 256.0).astype(jnp.float16), DP, axis=0, tiled=False)
    return (moment[None], gathered.astype(F32) * (1.0 / 256.0))


def solution(mesh):
    split = Mesh(mesh.devices.reshape(4, 2, 4, 8), ("y", "core", "x", "z"))
    placed = (P(None, DP, None), P(None, EXPERT, DP), P(DP, EXPERT, None), P())
    return jax.shard_map(
        body,
        mesh=split,
        in_specs=placed,
        out_specs=(P(DP, EXPERT, None), P(None, EXPERT, None)),
        check_vma=False,
    )
```

```python
import math

import jax
import jax.numpy as jnp
from jax import lax
from jax.experimental import pallas as pl
from jax.experimental.pallas import tpu as pltpu
from jax.sharding import Mesh
from jax.sharding import PartitionSpec as P

D = 7168
FF = 1024
TILE = 16
BLOCK = 128
UNIT = 16
NEEDED = 6

MOMENTUM_DECAY = 0.95
EPSILON = 1e-07
COEF_A = 3.4445
COEF_B = -4.775
COEF_C = 2.0315

DP = ("y", "core")
EXPERT = ("x", "z")

BF16 = jnp.bfloat16
F32 = jnp.float32


def split_two(value):
    high = value.astype(BF16)
    return high, (value - high.astype(F32)).astype(BF16)


def block_pairs(place):
    half = 0 if place < 2 else 1
    return [(0, 0), (0, 1), (0, 2), (0, 3), (0, 5), (1, 1), (1, 2), (1, 3), (half, 4 + half)]


def pieces_of(total, shape):
    first = total.astype(BF16).astype(F32)
    second = (total - first).astype(BF16).astype(F32)
    third = total - first - second
    rows = lax.broadcasted_iota(jnp.int32, shape, 0)
    tile = jnp.where(rows == 0, first, jnp.where(rows == 1, second, jnp.where(rows == 2, third, 0.0)))
    return tile.astype(BF16)


def column(place, block):
    return pl.ds(pl.multiple_of(lax.rem(2 * place + block, FF // BLOCK) * BLOCK, BLOCK), BLOCK)


def columns_kernel(place_ref, momentum_ref, *column_refs):
    for distance, column_ref in enumerate(column_refs, 1):
        for block in range(NEEDED):
            value = momentum_ref[:, column(place_ref[0] + distance, block)]
            column_ref[:, block * BLOCK : (block + 1) * BLOCK] = value.astype(BF16)


def fetched(sources, targets, semaphores):
    copies = [
        pltpu.make_async_copy(source, target, semaphores.at[at])
        for at, (source, target) in enumerate(zip(sources, targets))
    ]
    for copy in copies:
        copy.start()
    return copies


def gram_kernel(place_ref, counts_ref, hidden_ref, tokens_ref, *refs):
    count = (len(refs) - 4) // 2
    away_refs, moment_ref, cut_ref, needed_ref = refs[:count], *refs[count : count + 3]
    here_refs, semaphores = refs[count + 3 : -1], refs[-1]
    copies = fetched(away_refs, here_refs, semaphores)
    momentum_ref, other_refs = here_refs[0], here_refs[1:]
    groups, height, width = tokens_ref.shape
    place = place_ref[0]
    lanes = lax.broadcasted_iota(jnp.int32, (height, width), 1)

    def tokens_of(ref):
        kept = [jnp.where(lanes < counts_ref[g] * TILE, ref[g].astype(F32), 0.0) for g in range(groups)]
        return jnp.concatenate(kept, axis=1).astype(BF16)

    gradient = jnp.dot(
        tokens_of(tokens_ref), hidden_ref[...].reshape(groups * width, FF), preferred_element_type=F32
    )
    copies[0].wait()
    moment = MOMENTUM_DECAY * momentum_ref[...] + gradient
    moment_ref[...] = moment

    for g in range(groups):
        for block in range(NEEDED):
            needed_ref[g * width : (g + 1) * width, block * BLOCK : (block + 1) * BLOCK] = hidden_ref[
                g, :, column(place, block)
            ]
    values = [jnp.concatenate([moment_ref[:, column(place, block)] for block in range(NEEDED)], axis=1)]
    for copy in copies[1:]:
        copy.wait()
    others = len(other_refs) // 2
    for momentum_columns, other_tokens in zip(other_refs[:others], other_refs[others:]):
        gradient = jnp.dot(tokens_of(other_tokens), needed_ref[...], preferred_element_type=F32)
        values.append(MOMENTUM_DECAY * momentum_columns[...].astype(F32) + gradient)
    high, low = split_two(jnp.concatenate(values, axis=0))
    left = jnp.concatenate([high[:, : 2 * BLOCK], low[:, : 2 * BLOCK], high[:, : 2 * BLOCK]], axis=0).T
    right = jnp.concatenate([high, high, low], axis=0)
    strips = [
        jnp.dot(left[i * BLOCK : (i + 1) * BLOCK], right, preferred_element_type=F32).astype(BF16)
        for i in range(2)
    ]

    def block_of(i, j):
        return strips[i][:, j * BLOCK : (j + 1) * BLOCK]

    blocks = [block_of(i, j) for i, j in block_pairs(0)[:-1]]
    blocks.append(jnp.where(place < 2, block_of(*block_pairs(0)[-1]), block_of(*block_pairs(2)[-1])))
    per_device = cut_ref.shape[1] // UNIT - 1
    for unit in range(cut_ref.shape[0] * per_device):
        device, at = divmod(unit, per_device)
        block, row = divmod(unit * UNIT, BLOCK)
        cut_ref[device, at * UNIT : (at + 1) * UNIT] = blocks[block][row : row + UNIT]
    total = jnp.sum(jnp.sum(moment * moment, axis=0, keepdims=True), axis=1, keepdims=True)
    for device in range(cut_ref.shape[0]):
        cut_ref[device, per_device * UNIT :] = pieces_of(total, (UNIT, BLOCK))


def sum_kernel(parts_ref, copies_ref):
    total = parts_ref[0].astype(F32)
    for source in range(1, parts_ref.shape[0]):
        total = total + parts_ref[source].astype(F32)
    rows = total.shape[0] - UNIT
    squares = jnp.sum(total[rows:, 0:1], axis=0, keepdims=True)
    piece = total[:rows].astype(BF16)
    tile = pieces_of(squares, (UNIT, BLOCK))
    for target in range(copies_ref.shape[0]):
        copies_ref[target, :rows] = piece
        copies_ref[target, rows:] = tile


def polynomial_kernel(place_ref, moment_away_ref, *refs):
    *chunk_refs, update_ref, packed_ref, gram_ref, moment_ref, semaphores = refs
    copies = fetched([moment_away_ref], [moment_ref], semaphores)
    chunks = len(chunk_refs)
    pieces, height, _ = chunk_refs[0].shape
    rows = height - UNIT
    squares = jnp.zeros((1, 1), F32)
    for distance, chunk_ref in enumerate(chunk_refs):
        source = lax.rem(place_ref[0] - distance + chunks, chunks)
        for piece in range(pieces):
            packed_ref[source, piece * rows : (piece + 1) * rows] = chunk_ref[piece, :rows]
        squares = squares + jnp.sum(chunk_ref[0, rows:].astype(F32)[:, 0:1], axis=0, keepdims=True)
    factor = 1.0 / (jnp.sqrt(squares) + EPSILON)
    for source in range(chunks):
        for at, pair in enumerate(block_pairs(source)):
            i, j = ((2 * source + block) % (FF // BLOCK) for block in pair)
            block = packed_ref[source, at * BLOCK : (at + 1) * BLOCK]
            gram_ref[i * BLOCK : (i + 1) * BLOCK, j * BLOCK : (j + 1) * BLOCK] = block
            if i != j:
                gram_ref[j * BLOCK : (j + 1) * BLOCK, i * BLOCK : (i + 1) * BLOCK] = block.T

    def by_gram(value):
        rows = value.shape[0]
        both = jnp.dot(
            jnp.concatenate(split_two(value), axis=0), gram_ref[...], preferred_element_type=F32
        )
        return (both[:rows] + both[rows:]) * factor * factor

    def by_first(value):
        return COEF_A * value + by_gram(COEF_B * value + COEF_C * by_gram(value))

    def by_second_gram(value):
        return by_first(by_gram(by_first(value)))

    copies[0].wait()
    once = by_first(moment_ref[...] * factor)
    twice = COEF_A * once + by_second_gram(COEF_B * once + COEF_C * by_second_gram(once))
    update_ref[...] = twice * math.sqrt(max(FF, D))


def whole(memory_space=pltpu.VMEM):
    return pl.BlockSpec(memory_space=memory_space)


MIB = 1024 * 1024


def call(kernel, out_shape, inputs, scratch=(), scalars=0, away=(), mib=8):
    return pl.pallas_call(
        kernel,
        out_shape=out_shape,
        in_specs=[
            whole(pltpu.SMEM if at < scalars else pltpu.HBM if at in away else pltpu.VMEM)
            for at in range(len(inputs))
        ],
        out_specs=jax.tree.map(lambda _: whole(), out_shape),
        scratch_shapes=scratch,
        compiler_params=pltpu.CompilerParams(vmem_limit_bytes=mib * MIB),
        name=kernel.__name__.removesuffix("_kernel"),
    )(*inputs)


def shifted(value, axis, distance):
    size = lax.axis_size(axis)
    return lax.ppermute(value, axis, [(i, (i + distance) % size) for i in range(size)])


def body(hidden_token_tiles, gradient_token_tiles, momentum, filled_tile_count):
    along_x, along_z = lax.axis_size("x"), lax.axis_size("z")
    rows = momentum.shape[1]
    piece = len(block_pairs(0)) * BLOCK // along_z
    counts = lax.dynamic_index_in_dim(filled_tile_count, lax.axis_index(DP), 1, keepdims=False)
    place = lax.axis_index("x").astype(jnp.int32).reshape(1)
    distances = range(1, along_x)

    columns = call(
        columns_kernel,
        [jax.ShapeDtypeStruct((rows, NEEDED * BLOCK), BF16) for _ in distances],
        [place, momentum[0]],
        scalars=1,
    )
    columns, gradient_token_tiles = lax.optimization_barrier((columns, gradient_token_tiles))
    other_columns = [shifted(columns[k - 1], "x", k) for k in distances]
    tokens = lax.all_to_all(gradient_token_tiles, DP, 0, 0, tiled=True)
    other_columns[0], other_columns[-1], tokens, hidden_token_tiles = lax.optimization_barrier(
        (other_columns[0], other_columns[-1], tokens, hidden_token_tiles)
    )
    other_tokens = [shifted(tokens, "x", k) for k in distances]
    hidden = lax.all_to_all(hidden_token_tiles, DP, 0, 0, tiled=True)
    fetch = [
        pltpu.with_memory_space_constraint(value, pltpu.HBM)
        for value in [momentum[0]] + other_columns + other_tokens
    ]
    moment, cut = call(
        gram_kernel,
        (
            jax.ShapeDtypeStruct((rows, FF), F32),
            jax.ShapeDtypeStruct((along_z, piece + UNIT, BLOCK), BF16),
        ),
        [place, counts, hidden, tokens] + fetch,
        scratch=[pltpu.VMEM((hidden.shape[0] * hidden.shape[1], NEEDED * BLOCK), BF16)]
        + [pltpu.VMEM(value.shape, value.dtype) for value in fetch]
        + [pltpu.SemaphoreType.DMA((len(fetch),))],
        away=range(4, 4 + len(fetch)),
        scalars=2,
        mib=28,
    )
    copies = call(
        sum_kernel,
        jax.ShapeDtypeStruct((along_z, piece + UNIT, BLOCK), BF16),
        [lax.all_to_all(cut, "z", 0, 0, tiled=True)],
    )
    own = lax.all_to_all(copies, "z", 0, 0, tiled=True)
    update = call(
        polynomial_kernel,
        jax.ShapeDtypeStruct((rows, FF), F32),
        [place, pltpu.with_memory_space_constraint(moment, pltpu.HBM), own] + [shifted(own, "x", k) for k in distances],
        scratch=[
            pltpu.VMEM((along_x, along_z * piece, BLOCK), BF16),
            pltpu.VMEM((FF, FF), BF16),
            pltpu.VMEM((rows, FF), F32),
            pltpu.SemaphoreType.DMA((1,)),
        ],
        away=(1,),
        scalars=1,
        mib=20,
    )
    gathered = lax.all_gather((update * 256.0).astype(jnp.float16), DP, axis=0, tiled=False)
    return (moment[None], gathered.astype(F32) * (1.0 / 256.0))


def solution(mesh):
    split = Mesh(mesh.devices.reshape(4, 2, 4, 8), ("y", "core", "x", "z"))
    placed = (P(None, DP, None), P(None, EXPERT, DP), P(DP, EXPERT, None), P())
    return jax.shard_map(
        body,
        mesh=split,
        in_specs=placed,
        out_specs=(P(DP, EXPERT, None), P(None, EXPERT, None)),
        check_vma=False,
    )
```

```python
import math

import jax
import jax.numpy as jnp
from jax import lax
from jax.experimental import pallas as pl
from jax.experimental.pallas import tpu as pltpu
from jax.sharding import Mesh
from jax.sharding import PartitionSpec as P

D = 7168
FF = 1024
TILE = 16
BLOCK = 128
UNIT = 16
NEEDED = 6
CORES = 2

MOMENTUM_DECAY = 0.95
EPSILON = 1e-07
COEF_A = 3.4445
COEF_B = -4.775
COEF_C = 2.0315

DP = ("y", "core")
EXPERT = ("x", "z")

BF16 = jnp.bfloat16
F32 = jnp.float32


def split_two(value):
    high = value.astype(BF16)
    return high, (value - high.astype(F32)).astype(BF16)


def block_pairs(place):
    half = 0 if place < 2 else 1
    return [(0, 0), (0, 1), (0, 2), (0, 3), (0, 5), (1, 1), (1, 2), (1, 3), (half, 4 + half)]


def pieces_of(total, shape):
    first = total.astype(BF16).astype(F32)
    second = (total - first).astype(BF16).astype(F32)
    third = total - first - second
    rows = lax.broadcasted_iota(jnp.int32, shape, 0)
    tile = jnp.where(rows == 0, first, jnp.where(rows == 1, second, jnp.where(rows == 2, third, 0.0)))
    return tile.astype(BF16)


def column(place, block):
    return pl.ds(pl.multiple_of(lax.rem(2 * place + block, FF // BLOCK) * BLOCK, BLOCK), BLOCK)


def outgoing_kernel(place_ref, group_ref, momentum_ref, tokens_ref, *refs):
    *column_refs, kept_ref, sent_ref = refs
    chip, core = lax.div(group_ref[0], CORES), lax.rem(group_ref[0], CORES)
    chips = kept_ref.shape[0]
    for distance, column_ref in enumerate(column_refs, 1):
        for block in range(NEEDED):
            value = momentum_ref[:, column(place_ref[0] + distance, block)]
            column_ref[:, block * BLOCK : (block + 1) * BLOCK] = value.astype(BF16)
    for distance in range(chips):
        first = lax.rem(chip + distance, chips) * CORES
        kept_ref[distance] = tokens_ref[first + core]
        sent_ref[distance] = tokens_ref[first + 1 - core]


def fetched(sources, targets, semaphores):
    copies = [
        pltpu.make_async_copy(source, target, semaphores.at[at])
        for at, (source, target) in enumerate(zip(sources, targets))
    ]
    for copy in copies:
        copy.start()
    return copies


def gram_kernel(place_ref, group_ref, counts_ref, hidden_ref, tokens_ref, *refs):
    count = (len(refs) - 4) // 2
    away_refs, moment_ref, cut_ref, needed_ref = refs[:count], *refs[count : count + 3]
    here_refs, semaphores = refs[count + 3 : -1], refs[-1]
    copies = fetched(away_refs, here_refs, semaphores)
    momentum_ref, other_refs = here_refs[0], here_refs[1:]
    groups, height, width = tokens_ref.shape
    place = place_ref[0]
    lanes = lax.broadcasted_iota(jnp.int32, (height, width), 1)

    def tokens_of(ref):
        kept = []
        for g in range(groups):
            chip, core = divmod(g, CORES)
            distance = lax.rem(lax.div(group_ref[0], CORES) - chip + groups, groups // CORES)
            tokens = ref[CORES * distance + lax.rem(group_ref[0] + core, CORES)].astype(F32)
            kept.append(jnp.where(lanes < counts_ref[g] * TILE, tokens, 0.0).astype(BF16))
        return jnp.concatenate(kept, axis=1)

    gradient = jnp.dot(
        tokens_of(tokens_ref), hidden_ref[...].reshape(groups * width, FF), preferred_element_type=F32
    )
    copies[0].wait()
    moment = MOMENTUM_DECAY * momentum_ref[...] + gradient
    moment_ref[...] = moment

    for g in range(groups):
        for block in range(NEEDED):
            needed_ref[g * width : (g + 1) * width, block * BLOCK : (block + 1) * BLOCK] = hidden_ref[
                g, :, column(place, block)
            ]
    values = [jnp.concatenate([moment_ref[:, column(place, block)] for block in range(NEEDED)], axis=1)]
    for copy in copies[1:]:
        copy.wait()
    others = len(other_refs) // 2
    for momentum_columns, other_tokens in zip(other_refs[:others], other_refs[others:]):
        gradient = jnp.dot(tokens_of(other_tokens), needed_ref[...], preferred_element_type=F32)
        values.append(MOMENTUM_DECAY * momentum_columns[...].astype(F32) + gradient)
    high, low = split_two(jnp.concatenate(values, axis=0))
    left = jnp.concatenate([high[:, : 2 * BLOCK], low[:, : 2 * BLOCK], high[:, : 2 * BLOCK]], axis=0).T
    right = jnp.concatenate([high, high, low], axis=0)
    strips = [
        jnp.dot(left[i * BLOCK : (i + 1) * BLOCK], right, preferred_element_type=F32).astype(BF16)
        for i in range(2)
    ]

    def block_of(i, j):
        return strips[i][:, j * BLOCK : (j + 1) * BLOCK]

    blocks = [block_of(i, j) for i, j in block_pairs(0)[:-1]]
    blocks.append(jnp.where(place < 2, block_of(*block_pairs(0)[-1]), block_of(*block_pairs(2)[-1])))
    per_device = cut_ref.shape[1] // UNIT - 1
    for unit in range(cut_ref.shape[0] * per_device):
        device, at = divmod(unit, per_device)
        block, row = divmod(unit * UNIT, BLOCK)
        cut_ref[device, at * UNIT : (at + 1) * UNIT] = blocks[block][row : row + UNIT]
    total = jnp.sum(jnp.sum(moment * moment, axis=0, keepdims=True), axis=1, keepdims=True)
    for device in range(cut_ref.shape[0]):
        cut_ref[device, per_device * UNIT :] = pieces_of(total, (UNIT, BLOCK))


def sum_kernel(parts_ref, copies_ref):
    total = parts_ref[0].astype(F32)
    for source in range(1, parts_ref.shape[0]):
        total = total + parts_ref[source].astype(F32)
    rows = total.shape[0] - UNIT
    squares = jnp.sum(total[rows:, 0:1], axis=0, keepdims=True)
    piece = total[:rows].astype(BF16)
    tile = pieces_of(squares, (UNIT, BLOCK))
    for target in range(copies_ref.shape[0]):
        copies_ref[target, :rows] = piece
        copies_ref[target, rows:] = tile


def polynomial_kernel(place_ref, moment_away_ref, *refs):
    *chunk_refs, update_ref, packed_ref, gram_ref, moment_ref, semaphores = refs
    copies = fetched([moment_away_ref], [moment_ref], semaphores)
    chunks = len(chunk_refs)
    pieces, height, _ = chunk_refs[0].shape
    rows = height - UNIT
    squares = jnp.zeros((1, 1), F32)
    for distance, chunk_ref in enumerate(chunk_refs):
        source = lax.rem(place_ref[0] - distance + chunks, chunks)
        for piece in range(pieces):
            packed_ref[source, piece * rows : (piece + 1) * rows] = chunk_ref[piece, :rows]
        squares = squares + jnp.sum(chunk_ref[0, rows:].astype(F32)[:, 0:1], axis=0, keepdims=True)
    factor = 1.0 / (jnp.sqrt(squares) + EPSILON)
    for source in range(chunks):
        for at, pair in enumerate(block_pairs(source)):
            i, j = ((2 * source + block) % (FF // BLOCK) for block in pair)
            block = packed_ref[source, at * BLOCK : (at + 1) * BLOCK]
            gram_ref[i * BLOCK : (i + 1) * BLOCK, j * BLOCK : (j + 1) * BLOCK] = block
            if i != j:
                gram_ref[j * BLOCK : (j + 1) * BLOCK, i * BLOCK : (i + 1) * BLOCK] = block.T

    def by_gram(value):
        rows = value.shape[0]
        both = jnp.dot(
            jnp.concatenate(split_two(value), axis=0), gram_ref[...], preferred_element_type=F32
        )
        return (both[:rows] + both[rows:]) * factor * factor

    def by_first(value):
        return COEF_A * value + by_gram(COEF_B * value + COEF_C * by_gram(value))

    def by_second_gram(value):
        return by_first(by_gram(by_first(value)))

    copies[0].wait()
    once = by_first(moment_ref[...] * factor)
    twice = COEF_A * once + by_second_gram(COEF_B * once + COEF_C * by_second_gram(once))
    update_ref[...] = twice * math.sqrt(max(FF, D))


def whole(memory_space=pltpu.VMEM):
    return pl.BlockSpec(memory_space=memory_space)


MIB = 1024 * 1024


def call(kernel, out_shape, inputs, scratch=(), scalars=0, away=(), mib=8):
    return pl.pallas_call(
        kernel,
        out_shape=out_shape,
        in_specs=[
            whole(pltpu.SMEM if at < scalars else pltpu.HBM if at in away else pltpu.VMEM)
            for at in range(len(inputs))
        ],
        out_specs=jax.tree.map(lambda _: whole(), out_shape),
        scratch_shapes=scratch,
        compiler_params=pltpu.CompilerParams(vmem_limit_bytes=mib * MIB),
        name=kernel.__name__.removesuffix("_kernel"),
    )(*inputs)


def shifted(value, axis, distance):
    size = lax.axis_size(axis)
    return lax.ppermute(value, axis, [(i, (i + distance) % size) for i in range(size)])


def body(hidden_token_tiles, gradient_token_tiles, momentum, filled_tile_count):
    along_x, along_z = lax.axis_size("x"), lax.axis_size("z")
    rows = momentum.shape[1]
    piece = len(block_pairs(0)) * BLOCK // along_z
    group = lax.axis_index(DP).astype(jnp.int32)
    counts = lax.dynamic_index_in_dim(filled_tile_count, group, 1, keepdims=False)
    group = group.reshape(1)
    place = lax.axis_index("x").astype(jnp.int32).reshape(1)
    distances = range(1, along_x)
    along_y = lax.axis_size("y")

    hidden = lax.all_to_all(hidden_token_tiles, DP, 0, 0, tiled=True)
    half = jax.ShapeDtypeStruct((along_y, *gradient_token_tiles.shape[1:]), BF16)
    *columns, kept, sent = call(
        outgoing_kernel,
        [jax.ShapeDtypeStruct((rows, NEEDED * BLOCK), BF16) for _ in distances] + [half, half],
        [place, group, momentum[0], gradient_token_tiles],
        scalars=2,
    )
    other_columns = [shifted(columns[k - 1], "x", k) for k in distances]
    both = jnp.stack([kept, shifted(sent, "core", 1)], axis=1)
    tokens = jnp.concatenate([both[0]] + [shifted(both[k], "y", k) for k in range(1, along_y)])
    *other_columns, tokens = lax.optimization_barrier((*other_columns, tokens))
    other_tokens = [shifted(tokens, "x", k) for k in distances]
    fetch = [
        pltpu.with_memory_space_constraint(value, pltpu.HBM)
        for value in [momentum[0]] + other_columns + other_tokens
    ]
    moment, cut = call(
        gram_kernel,
        (
            jax.ShapeDtypeStruct((rows, FF), F32),
            jax.ShapeDtypeStruct((along_z, piece + UNIT, BLOCK), BF16),
        ),
        [place, group, counts, hidden, tokens] + fetch,
        scratch=[pltpu.VMEM((hidden.shape[0] * hidden.shape[1], NEEDED * BLOCK), BF16)]
        + [pltpu.VMEM(value.shape, value.dtype) for value in fetch]
        + [pltpu.SemaphoreType.DMA((len(fetch),))],
        away=range(5, 5 + len(fetch)),
        scalars=3,
        mib=28,
    )
    copies = call(
        sum_kernel,
        jax.ShapeDtypeStruct((along_z, piece + UNIT, BLOCK), BF16),
        [lax.all_to_all(cut, "z", 0, 0, tiled=True)],
    )
    own = lax.all_to_all(copies, "z", 0, 0, tiled=True)
    update = call(
        polynomial_kernel,
        jax.ShapeDtypeStruct((rows, FF), F32),
        [place, pltpu.with_memory_space_constraint(moment, pltpu.HBM), own] + [shifted(own, "x", k) for k in distances],
        scratch=[
            pltpu.VMEM((along_x, along_z * piece, BLOCK), BF16),
            pltpu.VMEM((FF, FF), BF16),
            pltpu.VMEM((rows, FF), F32),
            pltpu.SemaphoreType.DMA((1,)),
        ],
        away=(1,),
        scalars=1,
        mib=20,
    )
    gathered = lax.all_gather((update * 256.0).astype(jnp.float16), DP, axis=0, tiled=False)
    return (moment[None], gathered.astype(F32) * (1.0 / 256.0))


def solution(mesh):
    split = Mesh(mesh.devices.reshape(4, 2, 4, 8), ("y", "core", "x", "z"))
    placed = (P(None, DP, None), P(None, EXPERT, DP), P(DP, EXPERT, None), P())
    return jax.shard_map(
        body,
        mesh=split,
        in_specs=placed,
        out_specs=(P(DP, EXPERT, None), P(None, EXPERT, None)),
        check_vma=False,
    )
```

```python
import math

import jax
import jax.numpy as jnp
from jax import lax
from jax.experimental import pallas as pl
from jax.experimental.pallas import tpu as pltpu
from jax.sharding import Mesh
from jax.sharding import PartitionSpec as P

D = 7168
FF = 1024
TILE = 16
BLOCK = 128
UNIT = 16
NEEDED = 6
CORES = 2

MOMENTUM_DECAY = 0.95
EPSILON = 1e-07
COEF_A = 3.4445
COEF_B = -4.775
COEF_C = 2.0315

DP = ("y", "core")
EXPERT = ("x", "z")

BF16 = jnp.bfloat16
F32 = jnp.float32


def split_two(value):
    high = value.astype(BF16)
    return high, (value - high.astype(F32)).astype(BF16)


def block_pairs(place):
    half = 0 if place < 2 else 1
    return [(0, 0), (0, 1), (0, 2), (0, 3), (0, 5), (1, 1), (1, 2), (1, 3), (half, 4 + half)]


def pieces_of(total, shape):
    first = total.astype(BF16).astype(F32)
    second = (total - first).astype(BF16).astype(F32)
    third = total - first - second
    rows = lax.broadcasted_iota(jnp.int32, shape, 0)
    tile = jnp.where(rows == 0, first, jnp.where(rows == 1, second, jnp.where(rows == 2, third, 0.0)))
    return tile.astype(BF16)


def column(place, block):
    return pl.ds(pl.multiple_of(lax.rem(2 * place + block, FF // BLOCK) * BLOCK, BLOCK), BLOCK)


def outgoing_kernel(place_ref, group_ref, momentum_ref, tokens_ref, *refs):
    *column_refs, kept_ref, sent_ref = refs
    chip, core = lax.div(group_ref[0], CORES), lax.rem(group_ref[0], CORES)
    chips = kept_ref.shape[0]
    for distance, column_ref in enumerate(column_refs, 1):
        for block in range(NEEDED):
            value = momentum_ref[:, column(place_ref[0] + distance, block)]
            column_ref[:, block * BLOCK : (block + 1) * BLOCK] = value.astype(BF16)
    for distance in range(chips):
        first = lax.rem(chip + distance, chips) * CORES
        kept_ref[distance] = tokens_ref[first + core]
        sent_ref[distance] = tokens_ref[first + 1 - core]


def fetched(sources, targets, semaphores):
    copies = [
        pltpu.make_async_copy(source, target, semaphores.at[at])
        for at, (source, target) in enumerate(zip(sources, targets))
    ]
    for copy in copies:
        copy.start()
    return copies


def gram_kernel(place_ref, group_ref, counts_ref, hidden_ref, tokens_ref, *refs):
    count = (len(refs) - 4) // 2
    away_refs, moment_ref, cut_ref, needed_ref = refs[:count], *refs[count : count + 3]
    here_refs, semaphores = refs[count + 3 : -1], refs[-1]
    copies = fetched(away_refs, here_refs, semaphores)
    momentum_ref, other_refs = here_refs[0], here_refs[1:]
    groups, height, width = tokens_ref.shape
    place = place_ref[0]
    lanes = lax.broadcasted_iota(jnp.int32, (height, width), 1)

    def tokens_of(ref):
        kept = []
        for g in range(groups):
            chip, core = divmod(g, CORES)
            distance = lax.rem(lax.div(group_ref[0], CORES) - chip + groups, groups // CORES)
            tokens = ref[CORES * distance + lax.rem(group_ref[0] + core, CORES)].astype(F32)
            kept.append(jnp.where(lanes < counts_ref[g] * TILE, tokens, 0.0).astype(BF16))
        return jnp.concatenate(kept, axis=1)

    gradient = jnp.dot(
        tokens_of(tokens_ref), hidden_ref[...].reshape(groups * width, FF), preferred_element_type=F32
    )
    copies[0].wait()
    moment = MOMENTUM_DECAY * momentum_ref[...] + gradient
    moment_ref[...] = moment

    for g in range(groups):
        for block in range(NEEDED):
            needed_ref[g * width : (g + 1) * width, block * BLOCK : (block + 1) * BLOCK] = hidden_ref[
                g, :, column(place, block)
            ]
    values = [jnp.concatenate([moment_ref[:, column(place, block)] for block in range(NEEDED)], axis=1)]
    for copy in copies[1:]:
        copy.wait()
    others = len(other_refs) // 2
    for momentum_columns, other_tokens in zip(other_refs[:others], other_refs[others:]):
        gradient = jnp.dot(tokens_of(other_tokens), needed_ref[...], preferred_element_type=F32)
        values.append(MOMENTUM_DECAY * momentum_columns[...].astype(F32) + gradient)
    high, low = split_two(jnp.concatenate(values, axis=0))
    left = jnp.concatenate([high[:, : 2 * BLOCK], low[:, : 2 * BLOCK], high[:, : 2 * BLOCK]], axis=0).T
    right = jnp.concatenate([high, high, low], axis=0)
    strips = [
        jnp.dot(left[i * BLOCK : (i + 1) * BLOCK], right, preferred_element_type=F32).astype(BF16)
        for i in range(2)
    ]

    def block_of(i, j):
        return strips[i][:, j * BLOCK : (j + 1) * BLOCK]

    blocks = [block_of(i, j) for i, j in block_pairs(0)[:-1]]
    blocks.append(jnp.where(place < 2, block_of(*block_pairs(0)[-1]), block_of(*block_pairs(2)[-1])))
    per_device = cut_ref.shape[1] // UNIT - 1
    for unit in range(cut_ref.shape[0] * per_device):
        device, at = divmod(unit, per_device)
        block, row = divmod(unit * UNIT, BLOCK)
        cut_ref[device, at * UNIT : (at + 1) * UNIT] = blocks[block][row : row + UNIT]
    total = jnp.sum(jnp.sum(moment * moment, axis=0, keepdims=True), axis=1, keepdims=True)
    for device in range(cut_ref.shape[0]):
        cut_ref[device, per_device * UNIT :] = pieces_of(total, (UNIT, BLOCK))


def sum_kernel(parts_ref, copies_ref):
    total = parts_ref[0].astype(F32)
    for source in range(1, parts_ref.shape[0]):
        total = total + parts_ref[source].astype(F32)
    rows = total.shape[0] - UNIT
    squares = jnp.sum(total[rows:, 0:1], axis=0, keepdims=True)
    piece = total[:rows].astype(BF16)
    tile = pieces_of(squares, (UNIT, BLOCK))
    for target in range(copies_ref.shape[0]):
        copies_ref[target, :rows] = piece
        copies_ref[target, rows:] = tile


def polynomial_kernel(place_ref, moment_away_ref, *refs):
    *chunk_refs, update_ref, packed_ref, gram_ref, moment_ref, semaphores = refs
    copies = fetched([moment_away_ref], [moment_ref], semaphores)
    chunks = len(chunk_refs)
    pieces, height, _ = chunk_refs[0].shape
    rows = height - UNIT
    squares = jnp.zeros((1, 1), F32)
    for distance, chunk_ref in enumerate(chunk_refs):
        source = lax.rem(place_ref[0] - distance + chunks, chunks)
        for piece in range(pieces):
            packed_ref[source, piece * rows : (piece + 1) * rows] = chunk_ref[piece, :rows]
        squares = squares + jnp.sum(chunk_ref[0, rows:].astype(F32)[:, 0:1], axis=0, keepdims=True)
    factor = 1.0 / (jnp.sqrt(squares) + EPSILON)
    for source in range(chunks):
        for at, pair in enumerate(block_pairs(source)):
            i, j = ((2 * source + block) % (FF // BLOCK) for block in pair)
            block = packed_ref[source, at * BLOCK : (at + 1) * BLOCK]
            gram_ref[i * BLOCK : (i + 1) * BLOCK, j * BLOCK : (j + 1) * BLOCK] = block
            if i != j:
                gram_ref[j * BLOCK : (j + 1) * BLOCK, i * BLOCK : (i + 1) * BLOCK] = block.T

    def by_gram(value):
        rows = value.shape[0]
        both = jnp.dot(
            jnp.concatenate(split_two(value), axis=0), gram_ref[...], preferred_element_type=F32
        )
        return (both[:rows] + both[rows:]) * factor * factor

    def by_first(value):
        return COEF_A * value + by_gram(COEF_B * value + COEF_C * by_gram(value))

    def by_second_gram(value):
        return by_first(by_gram(by_first(value)))

    copies[0].wait()
    once = by_first(moment_ref[...] * factor)
    twice = COEF_A * once + by_second_gram(COEF_B * once + COEF_C * by_second_gram(once))
    update_ref[...] = twice * math.sqrt(max(FF, D))


def whole(memory_space=pltpu.VMEM):
    return pl.BlockSpec(memory_space=memory_space)


MIB = 1024 * 1024


def call(kernel, out_shape, inputs, scratch=(), scalars=0, away=(), mib=8):
    return pl.pallas_call(
        kernel,
        out_shape=out_shape,
        in_specs=[
            whole(pltpu.SMEM if at < scalars else pltpu.HBM if at in away else pltpu.VMEM)
            for at in range(len(inputs))
        ],
        out_specs=jax.tree.map(lambda _: whole(), out_shape),
        scratch_shapes=scratch,
        compiler_params=pltpu.CompilerParams(vmem_limit_bytes=mib * MIB),
        name=kernel.__name__.removesuffix("_kernel"),
    )(*inputs)


def shifted(value, axis, distance):
    size = lax.axis_size(axis)
    return lax.ppermute(value, axis, [(i, (i + distance) % size) for i in range(size)])


def body(hidden_token_tiles, gradient_token_tiles, momentum, filled_tile_count):
    along_x, along_z = lax.axis_size("x"), lax.axis_size("z")
    rows = momentum.shape[1]
    piece = len(block_pairs(0)) * BLOCK // along_z
    group = lax.axis_index(DP).astype(jnp.int32)
    counts = lax.dynamic_index_in_dim(filled_tile_count, group, 1, keepdims=False)
    group = group.reshape(1)
    place = lax.axis_index("x").astype(jnp.int32).reshape(1)
    distances = range(1, along_x)
    along_y = lax.axis_size("y")

    half = jax.ShapeDtypeStruct((along_y, *gradient_token_tiles.shape[1:]), BF16)
    *columns, kept, sent = call(
        outgoing_kernel,
        [jax.ShapeDtypeStruct((rows, NEEDED * BLOCK), BF16) for _ in distances] + [half, half],
        [place, group, momentum[0], gradient_token_tiles],
        scalars=2,
    )
    other_columns = [shifted(columns[k - 1], "x", k) for k in distances]
    both = jnp.stack([kept, shifted(sent, "core", 1)], axis=1)
    moved = [shifted(both[k], "y", k) for k in range(1, along_y)]
    *moved, other_columns[0], other_columns[-1], hidden_token_tiles = lax.optimization_barrier(
        (*moved, other_columns[0], other_columns[-1], hidden_token_tiles)
    )
    hidden = lax.all_to_all(hidden_token_tiles, DP, 0, 0, tiled=True)
    tokens = jnp.concatenate([both[0]] + moved)
    other_tokens = [shifted(tokens, "x", k) for k in distances]
    fetch = [
        pltpu.with_memory_space_constraint(value, pltpu.HBM)
        for value in [momentum[0]] + other_columns + other_tokens
    ]
    moment, cut = call(
        gram_kernel,
        (
            jax.ShapeDtypeStruct((rows, FF), F32),
            jax.ShapeDtypeStruct((along_z, piece + UNIT, BLOCK), BF16),
        ),
        [place, group, counts, hidden, tokens] + fetch,
        scratch=[pltpu.VMEM((hidden.shape[0] * hidden.shape[1], NEEDED * BLOCK), BF16)]
        + [pltpu.VMEM(value.shape, value.dtype) for value in fetch]
        + [pltpu.SemaphoreType.DMA((len(fetch),))],
        away=range(5, 5 + len(fetch)),
        scalars=3,
        mib=28,
    )
    copies = call(
        sum_kernel,
        jax.ShapeDtypeStruct((along_z, piece + UNIT, BLOCK), BF16),
        [lax.all_to_all(cut, "z", 0, 0, tiled=True)],
    )
    own = lax.all_to_all(copies, "z", 0, 0, tiled=True)
    update = call(
        polynomial_kernel,
        jax.ShapeDtypeStruct((rows, FF), F32),
        [place, pltpu.with_memory_space_constraint(moment, pltpu.HBM), own] + [shifted(own, "x", k) for k in distances],
        scratch=[
            pltpu.VMEM((along_x, along_z * piece, BLOCK), BF16),
            pltpu.VMEM((FF, FF), BF16),
            pltpu.VMEM((rows, FF), F32),
            pltpu.SemaphoreType.DMA((1,)),
        ],
        away=(1,),
        scalars=1,
        mib=20,
    )
    gathered = lax.all_gather((update * 256.0).astype(jnp.float16), DP, axis=0, tiled=False)
    return (moment[None], gathered.astype(F32) * (1.0 / 256.0))


def solution(mesh):
    split = Mesh(mesh.devices.reshape(4, 2, 4, 8), ("y", "core", "x", "z"))
    placed = (P(None, DP, None), P(None, EXPERT, DP), P(DP, EXPERT, None), P())
    return jax.shard_map(
        body,
        mesh=split,
        in_specs=placed,
        out_specs=(P(DP, EXPERT, None), P(None, EXPERT, None)),
        check_vma=False,
    )
```

```python
import math

import jax
import jax.numpy as jnp
from jax import lax
from jax.experimental import pallas as pl
from jax.experimental.pallas import tpu as pltpu
from jax.sharding import Mesh
from jax.sharding import PartitionSpec as P

D = 7168
FF = 1024
TILE = 16
BLOCK = 128
UNIT = 16
NEEDED = 6
CORES = 2

MOMENTUM_DECAY = 0.95
EPSILON = 1e-07
COEF_A = 3.4445
COEF_B = -4.775
COEF_C = 2.0315

DP = ("y", "core")
EXPERT = ("x", "z_pair", "z_low")

BF16 = jnp.bfloat16
F32 = jnp.float32


def split_two(value):
    high = value.astype(BF16)
    return high, (value - high.astype(F32)).astype(BF16)


def block_pairs(place):
    half = 0 if place < 2 else 1
    return [(0, 0), (0, 1), (0, 2), (0, 3), (0, 5), (1, 1), (1, 2), (1, 3), (half, 4 + half)]


def pieces_of(total, shape):
    first = total.astype(BF16).astype(F32)
    second = (total - first).astype(BF16).astype(F32)
    third = total - first - second
    rows = lax.broadcasted_iota(jnp.int32, shape, 0)
    tile = jnp.where(rows == 0, first, jnp.where(rows == 1, second, jnp.where(rows == 2, third, 0.0)))
    return tile.astype(BF16)


def column(place, block):
    return pl.ds(pl.multiple_of(lax.rem(2 * place + block, FF // BLOCK) * BLOCK, BLOCK), BLOCK)


def outgoing_kernel(place_ref, group_ref, momentum_away_ref, tokens_ref, *refs):
    *column_refs, kept_ref, sent_ref, momentum_ref, semaphores = refs
    chip, core = lax.div(group_ref[0], CORES), lax.rem(group_ref[0], CORES)
    chips = kept_ref.shape[0]
    sources, targets = [momentum_away_ref], [momentum_ref]
    for distance in range(chips):
        first = lax.rem(chip + distance, chips) * CORES
        sources += [tokens_ref.at[first + core], tokens_ref.at[first + 1 - core]]
        targets += [kept_ref.at[distance], sent_ref.at[distance]]
    copies = fetched(sources, targets, semaphores)
    copies[0].wait()
    for distance, column_ref in enumerate(column_refs, 1):
        for block in range(NEEDED):
            value = momentum_ref[:, column(place_ref[0] + distance, block)]
            column_ref[:, block * BLOCK : (block + 1) * BLOCK] = value.astype(BF16)
    for copy in copies[1:]:
        copy.wait()


def fetched(sources, targets, semaphores):
    copies = [
        pltpu.make_async_copy(source, target, semaphores.at[at])
        for at, (source, target) in enumerate(zip(sources, targets))
    ]
    for copy in copies:
        copy.start()
    return copies


def gram_kernel(place_ref, group_ref, counts_ref, hidden_ref, tokens_ref, *refs):
    count = (len(refs) - 4) // 2
    away_refs, moment_ref, cut_ref, needed_ref = refs[:count], *refs[count : count + 3]
    here_refs, semaphores = refs[count + 3 : -1], refs[-1]
    copies = fetched(away_refs, here_refs, semaphores)
    momentum_ref, other_refs = here_refs[0], here_refs[1:]
    groups, height, width = tokens_ref.shape
    place = place_ref[0]
    lanes = lax.broadcasted_iota(jnp.int32, (height, width), 1)

    def tokens_of(ref):
        kept = []
        for g in range(groups):
            chip, core = divmod(g, CORES)
            distance = lax.rem(lax.div(group_ref[0], CORES) - chip + groups, groups // CORES)
            tokens = ref[CORES * distance + lax.rem(group_ref[0] + core, CORES)].astype(F32)
            kept.append(jnp.where(lanes < counts_ref[g] * TILE, tokens, 0.0).astype(BF16))
        return jnp.concatenate(kept, axis=1)

    gradient = jnp.dot(
        tokens_of(tokens_ref), hidden_ref[...].reshape(groups * width, FF), preferred_element_type=F32
    )
    copies[0].wait()
    moment = MOMENTUM_DECAY * momentum_ref[...] + gradient
    moment_ref[...] = moment

    for g in range(groups):
        for block in range(NEEDED):
            needed_ref[g * width : (g + 1) * width, block * BLOCK : (block + 1) * BLOCK] = hidden_ref[
                g, :, column(place, block)
            ]
    values = [jnp.concatenate([moment_ref[:, column(place, block)] for block in range(NEEDED)], axis=1)]
    for copy in copies[1:]:
        copy.wait()
    others = len(other_refs) // 2
    for momentum_columns, other_tokens in zip(other_refs[:others], other_refs[others:]):
        gradient = jnp.dot(tokens_of(other_tokens), needed_ref[...], preferred_element_type=F32)
        values.append(MOMENTUM_DECAY * momentum_columns[...].astype(F32) + gradient)
    high, low = split_two(jnp.concatenate(values, axis=0))
    left = jnp.concatenate([high[:, : 2 * BLOCK], low[:, : 2 * BLOCK], high[:, : 2 * BLOCK]], axis=0).T
    right = jnp.concatenate([high, high, low], axis=0)
    strips = [
        jnp.dot(left[i * BLOCK : (i + 1) * BLOCK], right, preferred_element_type=F32).astype(BF16)
        for i in range(2)
    ]

    def block_of(i, j):
        return strips[i][:, j * BLOCK : (j + 1) * BLOCK]

    blocks = [block_of(i, j) for i, j in block_pairs(0)[:-1]]
    blocks.append(jnp.where(place < 2, block_of(*block_pairs(0)[-1]), block_of(*block_pairs(2)[-1])))
    pairs = cut_ref.shape[0]
    per_pair = cut_ref.shape[1] // UNIT - 1
    for unit in range(pairs * per_pair):
        pair, at = divmod(unit, per_pair)
        block, row = divmod(unit * UNIT, BLOCK)
        cut_ref[lax.rem(pair - place_ref[1] + pairs, pairs), at * UNIT : (at + 1) * UNIT] = blocks[block][
            row : row + UNIT
        ]
    total = jnp.sum(jnp.sum(moment * moment, axis=0, keepdims=True), axis=1, keepdims=True)
    for pair in range(pairs):
        cut_ref[pair, per_pair * UNIT :] = pieces_of(total, (UNIT, BLOCK))


def sum_kernel(*refs):
    *part_refs, sum_ref = refs
    total = part_refs[0][...].astype(F32)
    for part_ref in part_refs[1:]:
        total = total + part_ref[...].astype(F32)
    rows = total.shape[0] - UNIT
    sum_ref[:rows] = total[:rows].astype(BF16)
    squares = jnp.sum(total[rows:, 0:1], axis=0, keepdims=True)
    sum_ref[rows:] = pieces_of(squares, (UNIT, BLOCK))


def polynomial_kernel(place_ref, moment_away_ref, *refs):
    *chunk_refs, update_ref, packed_ref, gram_ref, moment_ref, semaphores = refs
    copies = fetched([moment_away_ref], [moment_ref], semaphores)
    chunks = len(chunk_refs)
    pieces, height, _ = chunk_refs[0].shape
    rows = height - UNIT
    squares = jnp.zeros((1, 1), F32)
    for distance, chunk_ref in enumerate(chunk_refs):
        source = lax.rem(place_ref[0] - distance + chunks, chunks)
        for piece in range(pieces):
            start = lax.rem(place_ref[1] - piece + pieces, pieces) * rows
            packed_ref[source, pl.ds(pl.multiple_of(start, UNIT), rows)] = chunk_ref[piece, :rows]
        squares = squares + jnp.sum(chunk_ref[0, rows:].astype(F32)[:, 0:1], axis=0, keepdims=True)
    factor = 1.0 / (jnp.sqrt(squares) + EPSILON)
    for source in range(chunks):
        for at, pair in enumerate(block_pairs(source)):
            i, j = ((2 * source + block) % (FF // BLOCK) for block in pair)
            block = packed_ref[source, at * BLOCK : (at + 1) * BLOCK]
            gram_ref[i * BLOCK : (i + 1) * BLOCK, j * BLOCK : (j + 1) * BLOCK] = block
            if i != j:
                gram_ref[j * BLOCK : (j + 1) * BLOCK, i * BLOCK : (i + 1) * BLOCK] = block.T

    def by_gram(value):
        rows = value.shape[0]
        both = jnp.dot(
            jnp.concatenate(split_two(value), axis=0), gram_ref[...], preferred_element_type=F32
        )
        return (both[:rows] + both[rows:]) * factor * factor

    def by_first(value):
        return COEF_A * value + by_gram(COEF_B * value + COEF_C * by_gram(value))

    def by_second_gram(value):
        return by_first(by_gram(by_first(value)))

    copies[0].wait()
    once = by_first(moment_ref[...] * factor)
    twice = COEF_A * once + by_second_gram(COEF_B * once + COEF_C * by_second_gram(once))
    update_ref[...] = twice * math.sqrt(max(FF, D))


def whole(memory_space=pltpu.VMEM):
    return pl.BlockSpec(memory_space=memory_space)


MIB = 1024 * 1024


def call(kernel, out_shape, inputs, scratch=(), scalars=0, away=(), mib=8):
    return pl.pallas_call(
        kernel,
        out_shape=out_shape,
        in_specs=[
            whole(pltpu.SMEM if at < scalars else pltpu.HBM if at in away else pltpu.VMEM)
            for at in range(len(inputs))
        ],
        out_specs=jax.tree.map(lambda _: whole(), out_shape),
        scratch_shapes=scratch,
        compiler_params=pltpu.CompilerParams(vmem_limit_bytes=mib * MIB),
        name=kernel.__name__.removesuffix("_kernel"),
    )(*inputs)


def shifted(value, axis, distance):
    size = lax.axis_size(axis)
    return lax.ppermute(value, axis, [(i, (i + distance) % size) for i in range(size)])


def body(hidden_token_tiles, gradient_token_tiles, momentum, filled_tile_count):
    along_x, pairs = lax.axis_size("x"), lax.axis_size("z_pair")
    rows = momentum.shape[1]
    piece = len(block_pairs(0)) * BLOCK // pairs
    group = lax.axis_index(DP).astype(jnp.int32)
    counts = lax.dynamic_index_in_dim(filled_tile_count, group, 1, keepdims=False)
    group = group.reshape(1)
    place = jnp.stack([lax.axis_index("x"), lax.axis_index("z_pair")]).astype(jnp.int32)
    distances = range(1, along_x)
    along_y = lax.axis_size("y")

    half = jax.ShapeDtypeStruct((along_y, *gradient_token_tiles.shape[1:]), BF16)
    *columns, kept, sent = call(
        outgoing_kernel,
        [jax.ShapeDtypeStruct((rows, NEEDED * BLOCK), BF16) for _ in distances] + [half, half],
        [place, group]
        + [pltpu.with_memory_space_constraint(value, pltpu.HBM) for value in (momentum[0], gradient_token_tiles)],
        scratch=[pltpu.VMEM((rows, FF), F32), pltpu.SemaphoreType.DMA((1 + CORES * along_y,))],
        away=(2, 3),
        scalars=2,
    )
    other_columns = [shifted(columns[k - 1], "x", k) for k in distances]
    both = jnp.stack([kept, shifted(sent, "core", 1)], axis=1)
    moved = [shifted(both[k], "y", k) for k in range(1, along_y)]
    *moved, other_columns[0], other_columns[-1], hidden_token_tiles = lax.optimization_barrier(
        (*moved, other_columns[0], other_columns[-1], hidden_token_tiles)
    )
    hidden = lax.all_to_all(hidden_token_tiles, DP, 0, 0, tiled=True)
    tokens = jnp.concatenate([both[0]] + moved)
    other_tokens = [shifted(tokens, "x", k) for k in distances]
    fetch = [
        pltpu.with_memory_space_constraint(value, pltpu.HBM)
        for value in [momentum[0]] + other_columns + other_tokens
    ]
    moment, parts = call(
        gram_kernel,
        (
            jax.ShapeDtypeStruct((rows, FF), F32),
            jax.ShapeDtypeStruct((pairs, piece + UNIT, BLOCK), BF16),
        ),
        [place, group, counts, hidden, tokens] + fetch,
        scratch=[pltpu.VMEM((hidden.shape[0] * hidden.shape[1], NEEDED * BLOCK), BF16)]
        + [pltpu.VMEM(value.shape, value.dtype) for value in fetch]
        + [pltpu.SemaphoreType.DMA((len(fetch),))],
        away=range(5, 5 + len(fetch)),
        scalars=3,
        mib=28,
    )
    summed = jax.ShapeDtypeStruct((piece + UNIT, BLOCK), BF16)
    part = call(sum_kernel, summed, [parts[0]] + [shifted(parts[k], "z_pair", k) for k in range(1, pairs)])
    part = call(sum_kernel, summed, [part, shifted(part, "z_low", 1)])
    own = jnp.stack([part] + [shifted(part, "z_pair", k) for k in range(1, pairs)])
    update = call(
        polynomial_kernel,
        jax.ShapeDtypeStruct((rows, FF), F32),
        [place, pltpu.with_memory_space_constraint(moment, pltpu.HBM), own] + [shifted(own, "x", k) for k in distances],
        scratch=[
            pltpu.VMEM((along_x, pairs * piece, BLOCK), BF16),
            pltpu.VMEM((FF, FF), BF16),
            pltpu.VMEM((rows, FF), F32),
            pltpu.SemaphoreType.DMA((1,)),
        ],
        away=(1,),
        scalars=1,
        mib=20,
    )
    gathered = lax.all_gather((update * 256.0).astype(jnp.float16), DP, axis=0, tiled=False)
    return (moment[None], gathered.astype(F32) * (1.0 / 256.0))


def solution(mesh):
    split = Mesh(mesh.devices.reshape(4, 2, 4, 4, 2), ("y", "core", "x", "z_pair", "z_low"))
    placed = (P(None, DP, None), P(None, EXPERT, DP), P(DP, EXPERT, None), P())
    return jax.shard_map(
        body,
        mesh=split,
        in_specs=placed,
        out_specs=(P(DP, EXPERT, None), P(None, EXPERT, None)),
        check_vma=False,
    )
```

```python
import math

import jax
import jax.numpy as jnp
from jax import lax
from jax.experimental import pallas as pl
from jax.experimental.pallas import tpu as pltpu
from jax.sharding import Mesh
from jax.sharding import PartitionSpec as P

D = 7168
FF = 1024
TILE = 16
BLOCK = 128
UNIT = 16
NEEDED = 6
CORES = 2

MOMENTUM_DECAY = 0.95
EPSILON = 1e-07
COEF_A = 3.4445
COEF_B = -4.775
COEF_C = 2.0315

DP = ("y", "core")
EXPERT = ("x", "z_pair", "z_low")

BF16 = jnp.bfloat16
F32 = jnp.float32


def split_two(value):
    high = value.astype(BF16)
    return high, (value - high.astype(F32)).astype(BF16)


def block_pairs(place):
    half = 0 if place < 2 else 1
    return [(0, 0), (0, 1), (0, 2), (0, 3), (0, 5), (1, 1), (1, 2), (1, 3), (half, 4 + half)]


def pieces_of(total, shape):
    first = total.astype(BF16).astype(F32)
    second = (total - first).astype(BF16).astype(F32)
    third = total - first - second
    rows = lax.broadcasted_iota(jnp.int32, shape, 0)
    tile = jnp.where(rows == 0, first, jnp.where(rows == 1, second, jnp.where(rows == 2, third, 0.0)))
    return tile.astype(BF16)


def column(place, block):
    return pl.ds(pl.multiple_of(lax.rem(2 * place + block, FF // BLOCK) * BLOCK, BLOCK), BLOCK)


def outgoing_kernel(place_ref, group_ref, counts_ref, momentum_away_ref, tokens_ref, *refs):
    *column_refs, kept_ref, sent_ref, momentum_ref, semaphores = refs
    chip, core = lax.div(group_ref[0], CORES), lax.rem(group_ref[0], CORES)
    chips = kept_ref.shape[0]
    sources, targets = [momentum_away_ref], [momentum_ref]
    for distance in range(chips):
        first = lax.rem(chip + distance, chips) * CORES
        sources += [tokens_ref.at[first + core], tokens_ref.at[first + 1 - core]]
        targets += [kept_ref.at[distance], sent_ref.at[distance]]
    copies = fetched(sources, targets, semaphores)
    copies[0].wait()
    for distance, column_ref in enumerate(column_refs, 1):
        for block in range(NEEDED):
            value = momentum_ref[:, column(place_ref[0] + distance, block)]
            column_ref[:, block * BLOCK : (block + 1) * BLOCK] = value.astype(BF16)
    for copy in copies[1:]:
        copy.wait()
    lanes = lax.broadcasted_iota(jnp.int32, tokens_ref.shape[1:], 1)
    for distance in range(chips):
        first = lax.rem(chip + distance, chips) * CORES
        for ref, expert in ((kept_ref, first + core), (sent_ref, first + 1 - core)):
            tokens = ref[distance].astype(F32)
            ref[distance] = jnp.where(lanes < counts_ref[expert] * TILE, tokens, 0.0).astype(BF16)


def fetched(sources, targets, semaphores):
    copies = [
        pltpu.make_async_copy(source, target, semaphores.at[at])
        for at, (source, target) in enumerate(zip(sources, targets))
    ]
    for copy in copies:
        copy.start()
    return copies


def gram_kernel(place_ref, group_ref, hidden_ref, tokens_ref, *refs):
    count = (len(refs) - 4) // 2
    away_refs, moment_ref, cut_ref, needed_ref = refs[:count], *refs[count : count + 3]
    here_refs, semaphores = refs[count + 3 : -1], refs[-1]
    copies = fetched(away_refs, here_refs, semaphores)
    momentum_ref, other_refs = here_refs[0], here_refs[1:]
    groups, _, width = tokens_ref.shape
    place = place_ref[0]

    def tokens_of(ref):
        kept = []
        for g in range(groups):
            chip, core = divmod(g, CORES)
            distance = lax.rem(lax.div(group_ref[0], CORES) - chip + groups, groups // CORES)
            kept.append(ref[CORES * distance + lax.rem(group_ref[0] + core, CORES)])
        return jnp.concatenate(kept, axis=1)

    gradient = jnp.dot(
        tokens_of(tokens_ref), hidden_ref[...].reshape(groups * width, FF), preferred_element_type=F32
    )
    copies[0].wait()
    moment = MOMENTUM_DECAY * momentum_ref[...] + gradient
    moment_ref[...] = moment

    for g in range(groups):
        for block in range(NEEDED):
            needed_ref[g * width : (g + 1) * width, block * BLOCK : (block + 1) * BLOCK] = hidden_ref[
                g, :, column(place, block)
            ]
    values = [jnp.concatenate([moment_ref[:, column(place, block)] for block in range(NEEDED)], axis=1)]
    for copy in copies[1:]:
        copy.wait()
    others = len(other_refs) // 2
    for momentum_columns, other_tokens in zip(other_refs[:others], other_refs[others:]):
        gradient = jnp.dot(tokens_of(other_tokens), needed_ref[...], preferred_element_type=F32)
        values.append(MOMENTUM_DECAY * momentum_columns[...].astype(F32) + gradient)
    high, low = split_two(jnp.concatenate(values, axis=0))
    left = jnp.concatenate([high[:, : 2 * BLOCK], low[:, : 2 * BLOCK], high[:, : 2 * BLOCK]], axis=0).T
    right = jnp.concatenate([high, high, low], axis=0)
    strips = [
        jnp.dot(left[i * BLOCK : (i + 1) * BLOCK], right, preferred_element_type=F32).astype(BF16)
        for i in range(2)
    ]

    def block_of(i, j):
        return strips[i][:, j * BLOCK : (j + 1) * BLOCK]

    blocks = [block_of(i, j) for i, j in block_pairs(0)[:-1]]
    blocks.append(jnp.where(place < 2, block_of(*block_pairs(0)[-1]), block_of(*block_pairs(2)[-1])))
    pairs = cut_ref.shape[0]
    per_pair = cut_ref.shape[1] // UNIT - 1
    for unit in range(pairs * per_pair):
        pair, at = divmod(unit, per_pair)
        block, row = divmod(unit * UNIT, BLOCK)
        cut_ref[lax.rem(pair - place_ref[1] + pairs, pairs), at * UNIT : (at + 1) * UNIT] = blocks[block][
            row : row + UNIT
        ]
    total = jnp.sum(jnp.sum(moment * moment, axis=0, keepdims=True), axis=1, keepdims=True)
    for pair in range(pairs):
        cut_ref[pair, per_pair * UNIT :] = pieces_of(total, (UNIT, BLOCK))


def sum_kernel(*refs):
    *part_refs, sum_ref = refs
    total = part_refs[0][...].astype(F32)
    for part_ref in part_refs[1:]:
        total = total + part_ref[...].astype(F32)
    rows = total.shape[0] - UNIT
    sum_ref[:rows] = total[:rows].astype(BF16)
    squares = jnp.sum(total[rows:, 0:1], axis=0, keepdims=True)
    sum_ref[rows:] = pieces_of(squares, (UNIT, BLOCK))


def polynomial_kernel(place_ref, moment_away_ref, *refs):
    *chunk_refs, update_ref, packed_ref, gram_ref, moment_ref, semaphores = refs
    copies = fetched([moment_away_ref], [moment_ref], semaphores)
    chunks = len(chunk_refs)
    pieces, height, _ = chunk_refs[0].shape
    rows = height - UNIT
    squares = jnp.zeros((1, 1), F32)
    for distance, chunk_ref in enumerate(chunk_refs):
        source = lax.rem(place_ref[0] - distance + chunks, chunks)
        for piece in range(pieces):
            start = lax.rem(place_ref[1] - piece + pieces, pieces) * rows
            packed_ref[source, pl.ds(pl.multiple_of(start, UNIT), rows)] = chunk_ref[piece, :rows]
        squares = squares + jnp.sum(chunk_ref[0, rows:].astype(F32)[:, 0:1], axis=0, keepdims=True)
    factor = 1.0 / (jnp.sqrt(squares) + EPSILON)
    for source in range(chunks):
        for at, pair in enumerate(block_pairs(source)):
            i, j = ((2 * source + block) % (FF // BLOCK) for block in pair)
            block = packed_ref[source, at * BLOCK : (at + 1) * BLOCK]
            gram_ref[i * BLOCK : (i + 1) * BLOCK, j * BLOCK : (j + 1) * BLOCK] = block
            if i != j:
                gram_ref[j * BLOCK : (j + 1) * BLOCK, i * BLOCK : (i + 1) * BLOCK] = block.T

    def by_gram(value):
        rows = value.shape[0]
        both = jnp.dot(
            jnp.concatenate(split_two(value), axis=0), gram_ref[...], preferred_element_type=F32
        )
        return both[:rows] + both[rows:]

    square = factor * factor
    linear, cubic = COEF_B * square, COEF_C * square * square

    def by_first(value):
        return COEF_A * value + by_gram(linear * value + cubic * by_gram(value))

    def by_second_gram(value):
        return by_first(by_gram(by_first(value)))

    copies[0].wait()
    once = by_first(moment_ref[...] * factor)
    twice = COEF_A * once + by_second_gram(linear * once + cubic * by_second_gram(once))
    update_ref[...] = twice * math.sqrt(max(FF, D))


def whole(memory_space=pltpu.VMEM):
    return pl.BlockSpec(memory_space=memory_space)


MIB = 1024 * 1024


def call(kernel, out_shape, inputs, scratch=(), scalars=0, away=(), mib=8):
    return pl.pallas_call(
        kernel,
        out_shape=out_shape,
        in_specs=[
            whole(pltpu.SMEM if at < scalars else pltpu.HBM if at in away else pltpu.VMEM)
            for at in range(len(inputs))
        ],
        out_specs=jax.tree.map(lambda _: whole(), out_shape),
        scratch_shapes=scratch,
        compiler_params=pltpu.CompilerParams(vmem_limit_bytes=mib * MIB),
        name=kernel.__name__.removesuffix("_kernel"),
    )(*inputs)


def shifted(value, axis, distance):
    size = lax.axis_size(axis)
    return lax.ppermute(value, axis, [(i, (i + distance) % size) for i in range(size)])


def body(hidden_token_tiles, gradient_token_tiles, momentum, filled_tile_count):
    along_x, pairs = lax.axis_size("x"), lax.axis_size("z_pair")
    rows = momentum.shape[1]
    piece = len(block_pairs(0)) * BLOCK // pairs
    group = lax.axis_index(DP).astype(jnp.int32)
    counts = lax.dynamic_index_in_dim(filled_tile_count, group, 0, keepdims=False)
    group = group.reshape(1)
    place = jnp.stack([lax.axis_index("x"), lax.axis_index("z_pair")]).astype(jnp.int32)
    distances = range(1, along_x)
    along_y = lax.axis_size("y")

    half = jax.ShapeDtypeStruct((along_y, *gradient_token_tiles.shape[1:]), BF16)
    *columns, kept, sent = call(
        outgoing_kernel,
        [jax.ShapeDtypeStruct((rows, NEEDED * BLOCK), BF16) for _ in distances] + [half, half],
        [place, group, counts]
        + [pltpu.with_memory_space_constraint(value, pltpu.HBM) for value in (momentum[0], gradient_token_tiles)],
        scratch=[pltpu.VMEM((rows, FF), F32), pltpu.SemaphoreType.DMA((1 + CORES * along_y,))],
        away=(3, 4),
        scalars=3,
    )
    other_columns = [shifted(columns[k - 1], "x", k) for k in distances]
    both = jnp.stack([kept, shifted(sent, "core", 1)], axis=1)
    moved = [shifted(both[k], "y", k) for k in range(1, along_y)]
    *moved, other_columns[0], other_columns[-1], hidden_token_tiles = lax.optimization_barrier(
        (*moved, other_columns[0], other_columns[-1], hidden_token_tiles)
    )
    hidden = lax.all_to_all(hidden_token_tiles, DP, 0, 0, tiled=True)
    tokens = jnp.concatenate([both[0]] + moved)
    other_tokens = [shifted(tokens, "x", k) for k in distances]
    fetch = [
        pltpu.with_memory_space_constraint(value, pltpu.HBM)
        for value in [momentum[0]] + other_columns + other_tokens
    ]
    moment, parts = call(
        gram_kernel,
        (
            jax.ShapeDtypeStruct((rows, FF), F32),
            jax.ShapeDtypeStruct((pairs, piece + UNIT, BLOCK), BF16),
        ),
        [place, group, hidden, tokens] + fetch,
        scratch=[pltpu.VMEM((hidden.shape[0] * hidden.shape[1], NEEDED * BLOCK), BF16)]
        + [pltpu.VMEM(value.shape, value.dtype) for value in fetch]
        + [pltpu.SemaphoreType.DMA((len(fetch),))],
        away=range(4, 4 + len(fetch)),
        scalars=2,
        mib=28,
    )
    summed = jax.ShapeDtypeStruct((piece + UNIT, BLOCK), BF16)
    part = call(sum_kernel, summed, [parts[0]] + [shifted(parts[k], "z_pair", k) for k in range(1, pairs)])
    part = call(sum_kernel, summed, [part, shifted(part, "z_low", 1)])
    own = jnp.stack([part] + [shifted(part, "z_pair", k) for k in range(1, pairs)])
    update = call(
        polynomial_kernel,
        jax.ShapeDtypeStruct((rows, FF), F32),
        [place, pltpu.with_memory_space_constraint(moment, pltpu.HBM), own] + [shifted(own, "x", k) for k in distances],
        scratch=[
            pltpu.VMEM((along_x, pairs * piece, BLOCK), BF16),
            pltpu.VMEM((FF, FF), BF16),
            pltpu.VMEM((rows, FF), F32),
            pltpu.SemaphoreType.DMA((1,)),
        ],
        away=(1,),
        scalars=1,
        mib=20,
    )
    gathered = lax.all_gather((update * 256.0).astype(jnp.float16), DP, axis=0, tiled=False)
    return (moment[None], gathered.astype(F32) * (1.0 / 256.0))


def solution(mesh):
    split = Mesh(mesh.devices.reshape(4, 2, 4, 4, 2), ("y", "core", "x", "z_pair", "z_low"))
    placed = (P(None, DP, None), P(None, EXPERT, DP), P(DP, EXPERT, None), P())
    return jax.shard_map(
        body,
        mesh=split,
        in_specs=placed,
        out_specs=(P(DP, EXPERT, None), P(None, EXPERT, None)),
        check_vma=False,
    )
```

```python
import math

import jax
import jax.numpy as jnp
from jax import lax
from jax.experimental import pallas as pl
from jax.experimental.pallas import tpu as pltpu
from jax.sharding import Mesh
from jax.sharding import PartitionSpec as P

D = 7168
FF = 1024
TILE = 16
BLOCK = 128
UNIT = 16
BAND = 32

MOMENTUM_DECAY = 0.95
EPSILON = 1e-07
COEF_A = 3.4445
COEF_B = -4.775
COEF_C = 2.0315

DP = ("y", "core")
EXPERT = ("x", "z_pair", "z_low")

BF16 = jnp.bfloat16
F32 = jnp.float32


def split_two(value):
    high = value.astype(BF16)
    return high, (value - high.astype(F32)).astype(BF16)


def block_pairs():
    count = FF // BLOCK
    return [(i, j) for i in range(count) for j in range(i, count)]


def pieces_of(total, shape):
    first = total.astype(BF16).astype(F32)
    second = (total - first).astype(BF16).astype(F32)
    third = total - first - second
    rows = lax.broadcasted_iota(jnp.int32, shape, 0)
    tile = jnp.where(rows == 0, first, jnp.where(rows == 1, second, jnp.where(rows == 2, third, 0.0)))
    return tile.astype(BF16)


def fetched(sources, targets, semaphores):
    copies = [
        pltpu.make_async_copy(source, target, semaphores.at[at])
        for at, (source, target) in enumerate(zip(sources, targets))
    ]
    for copy in copies:
        copy.start()
    return copies


def pack_kernel(hidden_ref, tokens_ref, packed_ref, semaphores):
    width = hidden_ref.shape[1]
    bands = tokens_ref.shape[1] // BAND
    sources, targets = [hidden_ref], [packed_ref.at[:, :width]]
    for at in range(FF // BLOCK):
        sources.append(tokens_ref.at[:, pl.ds(at % bands * BAND, BAND)])
        targets.append(packed_ref.at[:, pl.ds(width, BAND), pl.ds(at * BLOCK, BLOCK)])
    for copy in fetched(sources, targets, semaphores):
        copy.wait()


def gram_kernel(place_ref, counts_ref, tiles_ref, momentum_ref, moment_ref, packed_ref):
    groups, height, _ = tiles_ref.shape
    width = height - BAND
    lanes = lax.broadcasted_iota(jnp.int32, (BAND, BLOCK), 1)
    bands = momentum_ref.shape[0] // BAND

    def band(g, at):
        kept = tiles_ref[g, width:, at * BLOCK : (at + 1) * BLOCK].astype(F32)
        return jnp.where(lanes < counts_ref[g] * TILE, kept, 0.0).astype(BF16)

    tokens = jnp.concatenate(
        [jnp.concatenate([band(g, at) for at in range(bands)], axis=0) for g in range(groups)], axis=1
    )
    hidden = tiles_ref[:, :width].reshape(groups * width, FF)
    gradient = jnp.dot(tokens, hidden, preferred_element_type=F32)
    moment = MOMENTUM_DECAY * momentum_ref[...] + gradient
    moment_ref[...] = moment

    high, low = split_two(moment)
    left = jnp.concatenate([high, low, high], axis=0).T
    right = jnp.concatenate([high, high, low], axis=0)
    chunks = packed_ref.shape[0]
    per_chunk = len(block_pairs()) // chunks
    at = 0
    for i in range(FF // BLOCK):
        strip = jnp.dot(
            left[i * BLOCK : (i + 1) * BLOCK], right[:, i * BLOCK :], preferred_element_type=F32
        ).astype(BF16)
        for j in range(i, FF // BLOCK):
            chunk, place = divmod(at, per_chunk)
            packed_ref[
                lax.rem(chunk - place_ref[0] + chunks, chunks), place * BLOCK : (place + 1) * BLOCK, :
            ] = strip[:, (j - i) * BLOCK : (j - i + 1) * BLOCK]
            at += 1

    total = jnp.sum(jnp.sum(moment * moment, axis=0, keepdims=True), axis=1, keepdims=True)
    for chunk in range(chunks):
        packed_ref[chunk, per_chunk * BLOCK :, :] = pieces_of(total, (UNIT, BLOCK))


def middle_kernel(place_ref, *refs):
    *part_refs, cut_ref = refs
    pairs, height, _ = cut_ref.shape
    rows = height - UNIT
    total = part_refs[0][...].astype(F32)
    for part_ref in part_refs[1:]:
        total = total + part_ref[...].astype(F32)
    tile = pieces_of(jnp.sum(total[pairs * rows :, 0:1], axis=0, keepdims=True), (UNIT, BLOCK))
    for pair in range(pairs):
        at = lax.rem(pair - place_ref[1] + pairs, pairs)
        cut_ref[at, :rows] = total[pair * rows : (pair + 1) * rows].astype(BF16)
        cut_ref[at, rows:] = tile


def sum_kernel(*refs):
    *part_refs, sum_ref = refs
    total = part_refs[0][...].astype(F32)
    for part_ref in part_refs[1:]:
        total = total + part_ref[...].astype(F32)
    rows = total.shape[0] - UNIT
    sum_ref[:rows] = total[:rows].astype(BF16)
    squares = jnp.sum(total[rows:, 0:1], axis=0, keepdims=True)
    sum_ref[rows:] = pieces_of(squares, (UNIT, BLOCK))


def polynomial_kernel(place_ref, moment_away_ref, *refs):
    *chunk_refs, update_ref, packed_ref, gram_ref, moment_ref, semaphores = refs
    copies = fetched([moment_away_ref], [moment_ref], semaphores)
    chunks = len(chunk_refs)
    pieces, height, _ = chunk_refs[0].shape
    rows = height - UNIT
    squares = jnp.sum(chunk_refs[0][0, rows:].astype(F32)[:, 0:1], axis=0, keepdims=True)
    for distance, chunk_ref in enumerate(chunk_refs):
        source = lax.rem(place_ref[0] - distance + chunks, chunks)
        for piece in range(pieces):
            start = lax.rem(place_ref[1] - piece + pieces, pieces) * rows
            packed_ref[source, pl.ds(pl.multiple_of(start, UNIT), rows)] = chunk_ref[piece, :rows]
    factor = 1.0 / (jnp.sqrt(squares) + EPSILON)
    per_chunk = len(block_pairs()) // chunks
    for source in range(chunks):
        for at, (i, j) in enumerate(block_pairs()[source * per_chunk : (source + 1) * per_chunk]):
            block = packed_ref[source, at * BLOCK : (at + 1) * BLOCK]
            gram_ref[i * BLOCK : (i + 1) * BLOCK, j * BLOCK : (j + 1) * BLOCK] = block
            if i != j:
                gram_ref[j * BLOCK : (j + 1) * BLOCK, i * BLOCK : (i + 1) * BLOCK] = block.T

    def by_gram(value):
        rows = value.shape[0]
        both = jnp.dot(
            jnp.concatenate(split_two(value), axis=0), gram_ref[...], preferred_element_type=F32
        )
        return both[:rows] + both[rows:]

    square = factor * factor
    linear, cubic = COEF_B * square, COEF_C * square * square

    def by_first(value):
        return COEF_A * value + by_gram(linear * value + cubic * by_gram(value))

    def by_second_gram(value):
        return by_first(by_gram(by_first(value)))

    copies[0].wait()
    once = by_first(moment_ref[...] * factor)
    twice = COEF_A * once + by_second_gram(linear * once + cubic * by_second_gram(once))
    update_ref[...] = twice * math.sqrt(max(FF, D))


def whole(memory_space=pltpu.VMEM):
    return pl.BlockSpec(memory_space=memory_space)


MIB = 1024 * 1024


def call(kernel, out_shape, inputs, scratch=(), scalars=0, away=(), mib=8):
    return pl.pallas_call(
        kernel,
        out_shape=out_shape,
        in_specs=[
            whole(pltpu.SMEM if at < scalars else pltpu.HBM if at in away else pltpu.VMEM)
            for at in range(len(inputs))
        ],
        out_specs=jax.tree.map(lambda _: whole(), out_shape),
        scratch_shapes=scratch,
        compiler_params=pltpu.CompilerParams(vmem_limit_bytes=mib * MIB),
        name=kernel.__name__.removesuffix("_kernel"),
    )(*inputs)


def shifted(value, axis, distance):
    size = lax.axis_size(axis)
    return lax.ppermute(value, axis, [(i, (i + distance) % size) for i in range(size)])


def body(hidden_token_tiles, gradient_token_tiles, momentum, filled_tile_count):
    along_x, pairs = lax.axis_size("x"), lax.axis_size("z_pair")
    rows = momentum.shape[1]
    chunk = len(block_pairs()) * BLOCK // along_x
    piece = chunk // pairs
    experts, width, _ = hidden_token_tiles.shape
    counts = lax.dynamic_index_in_dim(filled_tile_count, lax.axis_index(DP), 1, keepdims=False)
    place = jnp.stack([lax.axis_index("x"), lax.axis_index("z_pair")]).astype(jnp.int32)

    packed = pl.pallas_call(
        pack_kernel,
        out_shape=jax.ShapeDtypeStruct((experts, width + BAND, FF), BF16),
        in_specs=[whole(pltpu.HBM), whole(pltpu.HBM)],
        out_specs=whole(pltpu.HBM),
        scratch_shapes=[pltpu.SemaphoreType.DMA((1 + FF // BLOCK,))],
        name="pack",
    )(*(pltpu.with_memory_space_constraint(value, pltpu.HBM) for value in (hidden_token_tiles, gradient_token_tiles)))
    tiles = lax.all_to_all(packed, DP, 0, 0, tiled=True)
    moment, parts = call(
        gram_kernel,
        (
            jax.ShapeDtypeStruct((rows, FF), F32),
            jax.ShapeDtypeStruct((along_x, chunk + UNIT, BLOCK), BF16),
        ),
        [place, counts, tiles, momentum[0]],
        scalars=2,
        mib=28,
    )
    parts = call(
        middle_kernel,
        jax.ShapeDtypeStruct((pairs, piece + UNIT, BLOCK), BF16),
        [place, parts[0]] + [shifted(parts[k], "x", k) for k in range(1, along_x)],
        scalars=1,
    )
    summed = jax.ShapeDtypeStruct((piece + UNIT, BLOCK), BF16)
    part = call(sum_kernel, summed, [parts[0]] + [shifted(parts[k], "z_pair", k) for k in range(1, pairs)])
    part = call(sum_kernel, summed, [part, shifted(part, "z_low", 1)])
    own = jnp.stack([part] + [shifted(part, "z_pair", k) for k in range(1, pairs)])
    update = call(
        polynomial_kernel,
        jax.ShapeDtypeStruct((rows, FF), F32),
        [place, pltpu.with_memory_space_constraint(moment, pltpu.HBM), own] + [shifted(own, "x", k) for k in range(1, along_x)],
        scratch=[
            pltpu.VMEM((along_x, pairs * piece, BLOCK), BF16),
            pltpu.VMEM((FF, FF), BF16),
            pltpu.VMEM((rows, FF), F32),
            pltpu.SemaphoreType.DMA((1,)),
        ],
        away=(1,),
        scalars=1,
        mib=20,
    )
    gathered = lax.all_gather((update * 256.0).astype(jnp.float16), DP, axis=0, tiled=False)
    return (moment[None], gathered.astype(F32) * (1.0 / 256.0))


def solution(mesh):
    split = Mesh(mesh.devices.reshape(4, 2, 4, 4, 2), ("y", "core", "x", "z_pair", "z_low"))
    placed = (P(None, DP, None), P(None, EXPERT, DP), P(DP, EXPERT, None), P())
    return jax.shard_map(
        body,
        mesh=split,
        in_specs=placed,
        out_specs=(P(DP, EXPERT, None), P(None, EXPERT, None)),
        check_vma=False,
    )
```

```python
import math

import jax
import jax.numpy as jnp
from jax import lax
from jax.experimental import pallas as pl
from jax.experimental.pallas import tpu as pltpu
from jax.sharding import Mesh
from jax.sharding import PartitionSpec as P

D = 7168
FF = 1024
TILE = 16
BLOCK = 128
UNIT = 16
NEEDED = 6
CORES = 2

MOMENTUM_DECAY = 0.95
EPSILON = 1e-07
COEF_A = 3.4445
COEF_B = -4.775
COEF_C = 2.0315

DP = ("y", "core")
EXPERT = ("x", "z_pair", "z_low")

BF16 = jnp.bfloat16
F32 = jnp.float32


def split_two(value):
    high = value.astype(BF16)
    return high, (value - high.astype(F32)).astype(BF16)


def block_pairs(place):
    half = 0 if place < 2 else 1
    return [(0, 0), (0, 1), (0, 2), (0, 3), (0, 5), (1, 1), (1, 2), (1, 3), (half, 4 + half)]


def pieces_of(total, shape):
    first = total.astype(BF16).astype(F32)
    second = (total - first).astype(BF16).astype(F32)
    third = total - first - second
    rows = lax.broadcasted_iota(jnp.int32, shape, 0)
    tile = jnp.where(rows == 0, first, jnp.where(rows == 1, second, jnp.where(rows == 2, third, 0.0)))
    return tile.astype(BF16)


def column(place, block):
    return pl.ds(pl.multiple_of(lax.rem(2 * place + block, FF // BLOCK) * BLOCK, BLOCK), BLOCK)


def tiles_kernel(group_ref, tokens_ref, kept_ref, sent_ref, semaphores):
    chip, core = lax.div(group_ref[0], CORES), lax.rem(group_ref[0], CORES)
    chips = kept_ref.shape[0]
    sources, targets = [], []
    for distance in range(chips):
        first = lax.rem(chip + distance, chips) * CORES
        sources += [tokens_ref.at[first + 1 - core], tokens_ref.at[first + core]]
        targets += [sent_ref.at[distance], kept_ref.at[distance]]
    for copy in fetched(sources, targets, semaphores):
        copy.wait()


def columns_kernel(place_ref, momentum_away_ref, *refs):
    *column_refs, momentum_ref, semaphores = refs
    for copy in fetched([momentum_away_ref], [momentum_ref], semaphores):
        copy.wait()
    for distance, column_ref in enumerate(column_refs, 1):
        for block in range(NEEDED):
            value = momentum_ref[:, column(place_ref[0] + distance, block)]
            column_ref[:, block * BLOCK : (block + 1) * BLOCK] = value.astype(BF16)


def fetched(sources, targets, semaphores):
    copies = [
        pltpu.make_async_copy(source, target, semaphores.at[at])
        for at, (source, target) in enumerate(zip(sources, targets))
    ]
    for copy in copies:
        copy.start()
    return copies


def gram_kernel(place_ref, group_ref, counts_ref, hidden_ref, tokens_ref, *refs):
    count = (len(refs) - 4) // 2
    away_refs, moment_ref, cut_ref, needed_ref = refs[:count], *refs[count : count + 3]
    here_refs, semaphores = refs[count + 3 : -1], refs[-1]
    copies = fetched(away_refs, here_refs, semaphores)
    momentum_ref, other_refs = here_refs[0], here_refs[1:]
    groups, height, width = tokens_ref.shape
    place = place_ref[0]
    lanes = lax.broadcasted_iota(jnp.int32, (height, width), 1)

    def tokens_of(ref):
        kept = []
        for g in range(groups):
            chip, core = divmod(g, CORES)
            distance = lax.rem(lax.div(group_ref[0], CORES) - chip + groups, groups // CORES)
            tokens = ref[CORES * distance + lax.rem(group_ref[0] + core, CORES)].astype(F32)
            kept.append(jnp.where(lanes < counts_ref[g] * TILE, tokens, 0.0).astype(BF16))
        return jnp.concatenate(kept, axis=1)

    gradient = jnp.dot(
        tokens_of(tokens_ref), hidden_ref[...].reshape(groups * width, FF), preferred_element_type=F32
    )
    copies[0].wait()
    moment = MOMENTUM_DECAY * momentum_ref[...] + gradient
    moment_ref[...] = moment

    for g in range(groups):
        for block in range(NEEDED):
            needed_ref[g * width : (g + 1) * width, block * BLOCK : (block + 1) * BLOCK] = hidden_ref[
                g, :, column(place, block)
            ]
    values = [jnp.concatenate([moment_ref[:, column(place, block)] for block in range(NEEDED)], axis=1)]
    for copy in copies[1:]:
        copy.wait()
    others = len(other_refs) // 2
    for momentum_columns, other_tokens in zip(other_refs[:others], other_refs[others:]):
        gradient = jnp.dot(tokens_of(other_tokens), needed_ref[...], preferred_element_type=F32)
        values.append(MOMENTUM_DECAY * momentum_columns[...].astype(F32) + gradient)
    high, low = split_two(jnp.concatenate(values, axis=0))
    left = jnp.concatenate([high[:, : 2 * BLOCK], low[:, : 2 * BLOCK], high[:, : 2 * BLOCK]], axis=0).T
    right = jnp.concatenate([high, high, low], axis=0)
    strips = [
        jnp.dot(left[i * BLOCK : (i + 1) * BLOCK], right, preferred_element_type=F32).astype(BF16)
        for i in range(2)
    ]

    def block_of(i, j):
        return strips[i][:, j * BLOCK : (j + 1) * BLOCK]

    blocks = [block_of(i, j) for i, j in block_pairs(0)[:-1]]
    blocks.append(jnp.where(place < 2, block_of(*block_pairs(0)[-1]), block_of(*block_pairs(2)[-1])))
    pairs = cut_ref.shape[0]
    per_pair = cut_ref.shape[1] // UNIT - 1
    for unit in range(pairs * per_pair):
        pair, at = divmod(unit, per_pair)
        block, row = divmod(unit * UNIT, BLOCK)
        cut_ref[lax.rem(pair - place_ref[1] + pairs, pairs), at * UNIT : (at + 1) * UNIT] = blocks[block][
            row : row + UNIT
        ]
    total = jnp.sum(jnp.sum(moment * moment, axis=0, keepdims=True), axis=1, keepdims=True)
    for pair in range(pairs):
        cut_ref[pair, per_pair * UNIT :] = pieces_of(total, (UNIT, BLOCK))


def sum_kernel(*refs):
    *part_refs, sum_ref = refs
    total = part_refs[0][...].astype(F32)
    for part_ref in part_refs[1:]:
        total = total + part_ref[...].astype(F32)
    rows = total.shape[0] - UNIT
    sum_ref[:rows] = total[:rows].astype(BF16)
    squares = jnp.sum(total[rows:, 0:1], axis=0, keepdims=True)
    sum_ref[rows:] = pieces_of(squares, (UNIT, BLOCK))


def polynomial_kernel(place_ref, moment_away_ref, *refs):
    *chunk_refs, update_ref, packed_ref, gram_ref, moment_ref, semaphores = refs
    copies = fetched([moment_away_ref], [moment_ref], semaphores)
    chunks = len(chunk_refs)
    pieces, height, _ = chunk_refs[0].shape
    rows = height - UNIT
    squares = jnp.zeros((1, 1), F32)
    for distance, chunk_ref in enumerate(chunk_refs):
        source = lax.rem(place_ref[0] - distance + chunks, chunks)
        for piece in range(pieces):
            start = lax.rem(place_ref[1] - piece + pieces, pieces) * rows
            packed_ref[source, pl.ds(pl.multiple_of(start, UNIT), rows)] = chunk_ref[piece, :rows]
        squares = squares + jnp.sum(chunk_ref[0, rows:].astype(F32)[:, 0:1], axis=0, keepdims=True)
    factor = 1.0 / (jnp.sqrt(squares) + EPSILON)
    for source in range(chunks):
        for at, pair in enumerate(block_pairs(source)):
            i, j = ((2 * source + block) % (FF // BLOCK) for block in pair)
            block = packed_ref[source, at * BLOCK : (at + 1) * BLOCK]
            gram_ref[i * BLOCK : (i + 1) * BLOCK, j * BLOCK : (j + 1) * BLOCK] = block
            if i != j:
                gram_ref[j * BLOCK : (j + 1) * BLOCK, i * BLOCK : (i + 1) * BLOCK] = block.T

    def by_gram(value):
        rows = value.shape[0]
        both = jnp.dot(
            jnp.concatenate(split_two(value), axis=0), gram_ref[...], preferred_element_type=F32
        )
        return (both[:rows] + both[rows:]) * factor * factor

    def by_first(value):
        return COEF_A * value + by_gram(COEF_B * value + COEF_C * by_gram(value))

    def by_second_gram(value):
        return by_first(by_gram(by_first(value)))

    copies[0].wait()
    once = by_first(moment_ref[...] * factor)
    twice = COEF_A * once + by_second_gram(COEF_B * once + COEF_C * by_second_gram(once))
    update_ref[...] = twice * math.sqrt(max(FF, D))


def whole(memory_space=pltpu.VMEM):
    return pl.BlockSpec(memory_space=memory_space)


MIB = 1024 * 1024


def call(kernel, out_shape, inputs, scratch=(), scalars=0, away=(), mib=8):
    return pl.pallas_call(
        kernel,
        out_shape=out_shape,
        in_specs=[
            whole(pltpu.SMEM if at < scalars else pltpu.HBM if at in away else pltpu.VMEM)
            for at in range(len(inputs))
        ],
        out_specs=jax.tree.map(lambda _: whole(), out_shape),
        scratch_shapes=scratch,
        compiler_params=pltpu.CompilerParams(vmem_limit_bytes=mib * MIB),
        name=kernel.__name__.removesuffix("_kernel"),
    )(*inputs)


def shifted(value, axis, distance):
    size = lax.axis_size(axis)
    return lax.ppermute(value, axis, [(i, (i + distance) % size) for i in range(size)])


def body(hidden_token_tiles, gradient_token_tiles, momentum, filled_tile_count):
    along_x, pairs = lax.axis_size("x"), lax.axis_size("z_pair")
    rows = momentum.shape[1]
    piece = len(block_pairs(0)) * BLOCK // pairs
    group = lax.axis_index(DP).astype(jnp.int32)
    counts = lax.dynamic_index_in_dim(filled_tile_count, group, 1, keepdims=False)
    group = group.reshape(1)
    place = jnp.stack([lax.axis_index("x"), lax.axis_index("z_pair")]).astype(jnp.int32)
    distances = range(1, along_x)
    along_y = lax.axis_size("y")

    half = jax.ShapeDtypeStruct((along_y, *gradient_token_tiles.shape[1:]), BF16)
    kept, sent = call(
        tiles_kernel,
        [half, half],
        [group, pltpu.with_memory_space_constraint(gradient_token_tiles, pltpu.HBM)],
        scratch=[pltpu.SemaphoreType.DMA((CORES * along_y,))],
        away=(1,),
        scalars=1,
    )
    columns = call(
        columns_kernel,
        [jax.ShapeDtypeStruct((rows, NEEDED * BLOCK), BF16) for _ in distances],
        [place, pltpu.with_memory_space_constraint(momentum[0], pltpu.HBM)],
        scratch=[pltpu.VMEM((rows, FF), F32), pltpu.SemaphoreType.DMA((1,))],
        away=(1,),
        scalars=1,
    )
    other_columns = [shifted(columns[k - 1], "x", k) for k in distances]
    both = jnp.stack([kept, shifted(sent, "core", 1)], axis=1)
    moved = [shifted(both[k], "y", k) for k in range(1, along_y)]
    *moved, other_columns[0], other_columns[-1], hidden_token_tiles = lax.optimization_barrier(
        (*moved, other_columns[0], other_columns[-1], hidden_token_tiles)
    )
    hidden = lax.all_to_all(hidden_token_tiles, DP, 0, 0, tiled=True)
    tokens = jnp.concatenate([both[0]] + moved)
    other_tokens = [shifted(tokens, "x", k) for k in distances]
    fetch = [
        pltpu.with_memory_space_constraint(value, pltpu.HBM)
        for value in [momentum[0]] + other_columns + other_tokens
    ]
    moment, parts = call(
        gram_kernel,
        (
            jax.ShapeDtypeStruct((rows, FF), F32),
            jax.ShapeDtypeStruct((pairs, piece + UNIT, BLOCK), BF16),
        ),
        [place, group, counts, hidden, tokens] + fetch,
        scratch=[pltpu.VMEM((hidden.shape[0] * hidden.shape[1], NEEDED * BLOCK), BF16)]
        + [pltpu.VMEM(value.shape, value.dtype) for value in fetch]
        + [pltpu.SemaphoreType.DMA((len(fetch),))],
        away=range(5, 5 + len(fetch)),
        scalars=3,
        mib=28,
    )
    summed = jax.ShapeDtypeStruct((piece + UNIT, BLOCK), BF16)
    part = call(sum_kernel, summed, [parts[0]] + [shifted(parts[k], "z_pair", k) for k in range(1, pairs)])
    part = call(sum_kernel, summed, [part, shifted(part, "z_low", 1)])
    own = jnp.stack([part] + [shifted(part, "z_pair", k) for k in range(1, pairs)])
    update = call(
        polynomial_kernel,
        jax.ShapeDtypeStruct((rows, FF), F32),
        [place, pltpu.with_memory_space_constraint(moment, pltpu.HBM), own] + [shifted(own, "x", k) for k in distances],
        scratch=[
            pltpu.VMEM((along_x, pairs * piece, BLOCK), BF16),
            pltpu.VMEM((FF, FF), BF16),
            pltpu.VMEM((rows, FF), F32),
            pltpu.SemaphoreType.DMA((1,)),
        ],
        away=(1,),
        scalars=1,
        mib=20,
    )
    gathered = lax.all_gather((update * 256.0).astype(jnp.float16), DP, axis=0, tiled=False)
    return (moment[None], gathered.astype(F32) * (1.0 / 256.0))


def solution(mesh):
    split = Mesh(mesh.devices.reshape(4, 2, 4, 4, 2), ("y", "core", "x", "z_pair", "z_low"))
    placed = (P(None, DP, None), P(None, EXPERT, DP), P(DP, EXPERT, None), P())
    return jax.shard_map(
        body,
        mesh=split,
        in_specs=placed,
        out_specs=(P(DP, EXPERT, None), P(None, EXPERT, None)),
        check_vma=False,
    )
```

```python
import math

import jax
import jax.numpy as jnp
from jax import lax
from jax.experimental import pallas as pl
from jax.experimental.pallas import tpu as pltpu
from jax.sharding import Mesh
from jax.sharding import PartitionSpec as P

D = 7168
FF = 1024
TILE = 16
BLOCK = 128
UNIT = 16
NEEDED = 6
CORES = 2

MOMENTUM_DECAY = 0.95
EPSILON = 1e-07
COEF_A = 3.4445
COEF_B = -4.775
COEF_C = 2.0315

DP = ("y", "core")
EXPERT = ("x", "z_pair", "z_low")

BF16 = jnp.bfloat16
F32 = jnp.float32


def split_two(value):
    high = value.astype(BF16)
    return high, (value - high.astype(F32)).astype(BF16)


def block_pairs(place):
    half = 0 if place < 2 else 1
    return [(0, 0), (0, 1), (0, 2), (0, 3), (0, 5), (1, 1), (1, 2), (1, 3), (half, 4 + half)]


def pieces_of(total, shape):
    first = total.astype(BF16).astype(F32)
    second = (total - first).astype(BF16).astype(F32)
    third = total - first - second
    rows = lax.broadcasted_iota(jnp.int32, shape, 0)
    tile = jnp.where(rows == 0, first, jnp.where(rows == 1, second, jnp.where(rows == 2, third, 0.0)))
    return tile.astype(BF16)


def column(place, block):
    return pl.ds(pl.multiple_of(lax.rem(2 * place + block, FF // BLOCK) * BLOCK, BLOCK), BLOCK)


def outgoing_kernel(place_ref, group_ref, momentum_away_ref, tokens_ref, *refs):
    *column_refs, kept_ref, sent_ref, momentum_ref, semaphores = refs
    chip, core = lax.div(group_ref[0], CORES), lax.rem(group_ref[0], CORES)
    chips = kept_ref.shape[0]
    sources, targets = [momentum_away_ref], [momentum_ref]
    for distance in range(chips):
        first = lax.rem(chip + distance, chips) * CORES
        sources += [tokens_ref.at[first + core], tokens_ref.at[first + 1 - core]]
        targets += [kept_ref.at[distance], sent_ref.at[distance]]
    copies = fetched(sources, targets, semaphores)
    copies[0].wait()
    for distance, column_ref in enumerate(column_refs, 1):
        for block in range(NEEDED):
            value = momentum_ref[:, column(place_ref[0] + distance, block)]
            column_ref[:, block * BLOCK : (block + 1) * BLOCK] = value.astype(BF16)
    for copy in copies[1:]:
        copy.wait()


def fetched(sources, targets, semaphores):
    copies = [
        pltpu.make_async_copy(source, target, semaphores.at[at])
        for at, (source, target) in enumerate(zip(sources, targets))
    ]
    for copy in copies:
        copy.start()
    return copies


def gram_kernel(place_ref, group_ref, counts_ref, hidden_ref, tokens_ref, *refs):
    count = (len(refs) - 3) // 3
    other_tokens, refs = refs[: count - 1], refs[count - 1 :]
    away_refs, moment_ref, cut_ref, needed_ref = refs[:count], *refs[count : count + 3]
    here_refs, semaphores = refs[count + 3 : -1], refs[-1]
    copies = fetched(away_refs, here_refs, semaphores)
    momentum_ref, other_refs = here_refs[0], here_refs[1:]
    groups, height, width = tokens_ref.shape
    place = place_ref[0]
    lanes = lax.broadcasted_iota(jnp.int32, (height, width), 1)

    def tokens_of(ref):
        kept = []
        for g in range(groups):
            chip, core = divmod(g, CORES)
            distance = lax.rem(lax.div(group_ref[0], CORES) - chip + groups, groups // CORES)
            tokens = ref[CORES * distance + lax.rem(group_ref[0] + core, CORES)].astype(F32)
            kept.append(jnp.where(lanes < counts_ref[g] * TILE, tokens, 0.0).astype(BF16))
        return jnp.concatenate(kept, axis=1)

    gradient = jnp.dot(
        tokens_of(tokens_ref), hidden_ref[...].reshape(groups * width, FF), preferred_element_type=F32
    )
    copies[0].wait()
    moment = MOMENTUM_DECAY * momentum_ref[...] + gradient
    moment_ref[...] = moment

    for g in range(groups):
        for block in range(NEEDED):
            needed_ref[g * width : (g + 1) * width, block * BLOCK : (block + 1) * BLOCK] = hidden_ref[
                g, :, column(place, block)
            ]
    values = [jnp.concatenate([moment_ref[:, column(place, block)] for block in range(NEEDED)], axis=1)]
    for copy in copies[1:]:
        copy.wait()
    for momentum_columns, tokens in zip(other_refs, other_tokens):
        gradient = jnp.dot(tokens_of(tokens), needed_ref[...], preferred_element_type=F32)
        values.append(MOMENTUM_DECAY * momentum_columns[...].astype(F32) + gradient)
    high, low = split_two(jnp.concatenate(values, axis=0))
    left = jnp.concatenate([high[:, : 2 * BLOCK], low[:, : 2 * BLOCK], high[:, : 2 * BLOCK]], axis=0).T
    right = jnp.concatenate([high, high, low], axis=0)
    strips = [
        jnp.dot(left[i * BLOCK : (i + 1) * BLOCK], right, preferred_element_type=F32).astype(BF16)
        for i in range(2)
    ]

    def block_of(i, j):
        return strips[i][:, j * BLOCK : (j + 1) * BLOCK]

    blocks = [block_of(i, j) for i, j in block_pairs(0)[:-1]]
    blocks.append(jnp.where(place < 2, block_of(*block_pairs(0)[-1]), block_of(*block_pairs(2)[-1])))
    pairs = cut_ref.shape[0]
    per_pair = cut_ref.shape[1] // UNIT - 1
    for unit in range(pairs * per_pair):
        pair, at = divmod(unit, per_pair)
        block, row = divmod(unit * UNIT, BLOCK)
        cut_ref[lax.rem(pair - place_ref[1] + pairs, pairs), at * UNIT : (at + 1) * UNIT] = blocks[block][
            row : row + UNIT
        ]
    total = jnp.sum(jnp.sum(moment * moment, axis=0, keepdims=True), axis=1, keepdims=True)
    for pair in range(pairs):
        cut_ref[pair, per_pair * UNIT :] = pieces_of(total, (UNIT, BLOCK))


def sum_kernel(*refs):
    *part_refs, sum_ref = refs
    total = part_refs[0][...].astype(F32)
    for part_ref in part_refs[1:]:
        total = total + part_ref[...].astype(F32)
    rows = total.shape[0] - UNIT
    sum_ref[:rows] = total[:rows].astype(BF16)
    squares = jnp.sum(total[rows:, 0:1], axis=0, keepdims=True)
    sum_ref[rows:] = pieces_of(squares, (UNIT, BLOCK))


def polynomial_kernel(place_ref, moment_away_ref, *refs):
    *chunk_refs, update_ref, packed_ref, gram_ref, moment_ref, semaphores = refs
    copies = fetched([moment_away_ref], [moment_ref], semaphores)
    chunks = len(chunk_refs)
    pieces, height, _ = chunk_refs[0].shape
    rows = height - UNIT
    squares = jnp.zeros((1, 1), F32)
    for distance, chunk_ref in enumerate(chunk_refs):
        source = lax.rem(place_ref[0] - distance + chunks, chunks)
        for piece in range(pieces):
            start = lax.rem(place_ref[1] - piece + pieces, pieces) * rows
            packed_ref[source, pl.ds(pl.multiple_of(start, UNIT), rows)] = chunk_ref[piece, :rows]
        squares = squares + jnp.sum(chunk_ref[0, rows:].astype(F32)[:, 0:1], axis=0, keepdims=True)
    factor = 1.0 / (jnp.sqrt(squares) + EPSILON)
    for source in range(chunks):
        for at, pair in enumerate(block_pairs(source)):
            i, j = ((2 * source + block) % (FF // BLOCK) for block in pair)
            block = packed_ref[source, at * BLOCK : (at + 1) * BLOCK]
            gram_ref[i * BLOCK : (i + 1) * BLOCK, j * BLOCK : (j + 1) * BLOCK] = block
            if i != j:
                gram_ref[j * BLOCK : (j + 1) * BLOCK, i * BLOCK : (i + 1) * BLOCK] = block.T

    def by_gram(value):
        rows = value.shape[0]
        both = jnp.dot(
            jnp.concatenate(split_two(value), axis=0), gram_ref[...], preferred_element_type=F32
        )
        return (both[:rows] + both[rows:]) * factor * factor

    def by_first(value):
        return COEF_A * value + by_gram(COEF_B * value + COEF_C * by_gram(value))

    def by_second_gram(value):
        return by_first(by_gram(by_first(value)))

    copies[0].wait()
    once = by_first(moment_ref[...] * factor)
    twice = COEF_A * once + by_second_gram(COEF_B * once + COEF_C * by_second_gram(once))
    update_ref[...] = twice * math.sqrt(max(FF, D))


def whole(memory_space=pltpu.VMEM):
    return pl.BlockSpec(memory_space=memory_space)


MIB = 1024 * 1024


def call(kernel, out_shape, inputs, scratch=(), scalars=0, away=(), mib=8):
    return pl.pallas_call(
        kernel,
        out_shape=out_shape,
        in_specs=[
            whole(pltpu.SMEM if at < scalars else pltpu.HBM if at in away else pltpu.VMEM)
            for at in range(len(inputs))
        ],
        out_specs=jax.tree.map(lambda _: whole(), out_shape),
        scratch_shapes=scratch,
        compiler_params=pltpu.CompilerParams(vmem_limit_bytes=mib * MIB),
        name=kernel.__name__.removesuffix("_kernel"),
    )(*inputs)


def shifted(value, axis, distance):
    size = lax.axis_size(axis)
    return lax.ppermute(value, axis, [(i, (i + distance) % size) for i in range(size)])


def body(hidden_token_tiles, gradient_token_tiles, momentum, filled_tile_count):
    along_x, pairs = lax.axis_size("x"), lax.axis_size("z_pair")
    rows = momentum.shape[1]
    piece = len(block_pairs(0)) * BLOCK // pairs
    group = lax.axis_index(DP).astype(jnp.int32)
    counts = lax.dynamic_index_in_dim(filled_tile_count, group, 1, keepdims=False)
    group = group.reshape(1)
    place = jnp.stack([lax.axis_index("x"), lax.axis_index("z_pair")]).astype(jnp.int32)
    distances = range(1, along_x)
    along_y = lax.axis_size("y")

    half = jax.ShapeDtypeStruct((along_y, *gradient_token_tiles.shape[1:]), BF16)
    *columns, kept, sent = call(
        outgoing_kernel,
        [jax.ShapeDtypeStruct((rows, NEEDED * BLOCK), BF16) for _ in distances] + [half, half],
        [place, group]
        + [pltpu.with_memory_space_constraint(value, pltpu.HBM) for value in (momentum[0], gradient_token_tiles)],
        scratch=[pltpu.VMEM((rows, FF), F32), pltpu.SemaphoreType.DMA((1 + CORES * along_y,))],
        away=(2, 3),
        scalars=2,
    )
    other_columns = [shifted(columns[k - 1], "x", k) for k in distances]
    both = jnp.stack([kept, shifted(sent, "core", 1)], axis=1)
    moved = [shifted(both[k], "y", k) for k in range(1, along_y)]
    *moved, other_columns[0], other_columns[-1], hidden_token_tiles = lax.optimization_barrier(
        (*moved, other_columns[0], other_columns[-1], hidden_token_tiles)
    )
    hidden = lax.all_to_all(hidden_token_tiles, DP, 0, 0, tiled=True)
    tokens = jnp.concatenate([both[0]] + moved)
    other_tokens = [shifted(tokens, "x", k) for k in distances]
    fetch = [
        pltpu.with_memory_space_constraint(value, pltpu.HBM)
        for value in [momentum[0]] + other_columns
    ]
    moment, parts = call(
        gram_kernel,
        (
            jax.ShapeDtypeStruct((rows, FF), F32),
            jax.ShapeDtypeStruct((pairs, piece + UNIT, BLOCK), BF16),
        ),
        [place, group, counts, hidden, tokens] + other_tokens + fetch,
        scratch=[pltpu.VMEM((hidden.shape[0] * hidden.shape[1], NEEDED * BLOCK), BF16)]
        + [pltpu.VMEM(value.shape, value.dtype) for value in fetch]
        + [pltpu.SemaphoreType.DMA((len(fetch),))],
        away=range(5 + len(other_tokens), 5 + len(other_tokens) + len(fetch)),
        scalars=3,
        mib=28,
    )
    summed = jax.ShapeDtypeStruct((piece + UNIT, BLOCK), BF16)
    part = call(sum_kernel, summed, [parts[0]] + [shifted(parts[k], "z_pair", k) for k in range(1, pairs)])
    part = call(sum_kernel, summed, [part, shifted(part, "z_low", 1)])
    own = jnp.stack([part] + [shifted(part, "z_pair", k) for k in range(1, pairs)])
    update = call(
        polynomial_kernel,
        jax.ShapeDtypeStruct((rows, FF), F32),
        [place, pltpu.with_memory_space_constraint(moment, pltpu.HBM), own] + [shifted(own, "x", k) for k in distances],
        scratch=[
            pltpu.VMEM((along_x, pairs * piece, BLOCK), BF16),
            pltpu.VMEM((FF, FF), BF16),
            pltpu.VMEM((rows, FF), F32),
            pltpu.SemaphoreType.DMA((1,)),
        ],
        away=(1,),
        scalars=1,
        mib=20,
    )
    gathered = lax.all_gather((update * 256.0).astype(jnp.float16), DP, axis=0, tiled=False)
    return (moment[None], gathered.astype(F32) * (1.0 / 256.0))


def solution(mesh):
    split = Mesh(mesh.devices.reshape(4, 2, 4, 4, 2), ("y", "core", "x", "z_pair", "z_low"))
    placed = (P(None, DP, None), P(None, EXPERT, DP), P(DP, EXPERT, None), P())
    return jax.shard_map(
        body,
        mesh=split,
        in_specs=placed,
        out_specs=(P(DP, EXPERT, None), P(None, EXPERT, None)),
        check_vma=False,
    )
```
